32 devices in a mesh: dp: 8 (over z, y), tensor: 4 (over x, core).
Axes of the slice: x: 2, y: 2, z: 4, core: 2. Of those that a mesh axis runs over, the one named last changes fastest.
Arguments:
- layer_input: bfloat16 [4096, 768], P(('dp', 'tensor')), may hold values from -6 to 6
- cotangent: bfloat16 [4096, 768], P(('dp', 'tensor')), may hold values from -6 to 6
- segments: int32 [4096], P('dp'), may hold values from 0 to 3, as said below
- positions: int32 [4096], P('dp'), may hold values from 0 to 508, as said below
- norm1_gain: float32 [768], replicated, may hold values from 0.1 to 1.9
- norm1_bias: float32 [768], replicated, may hold values from -1.5 to 1.5
- norm2_gain: float32 [768], replicated, may hold values from 0.1 to 1.9
- norm2_bias: float32 [768], replicated, may hold values from -1.5 to 1.5
- qkv_weight: bfloat16 [768, 3, 768], P('dp', None, 'tensor'), may hold values from -2.5 to 2.5
- qkv_bias: float32 [3, 768], P(None, 'tensor'), may hold values from -2.5 to 2.5
- out_weight: bfloat16 [768, 768], P('tensor', 'dp'), may hold values from -0.875 to 0.875
- fc1_weight: bfloat16 [768, 3072], P('dp', 'tensor'), may hold values from -0.21875 to 0.21875
- fc1_bias: float32 [3072], P('tensor'), may hold values from -2.5 to 2.5
- fc2_weight: bfloat16 [3072, 768], P('tensor', 'dp'), may hold values from -0.109375 to 0.109375
- out_bias: float32 [768], replicated, may hold values from -2.5 to 2.5
Outputs:
- activations: bfloat16 [4096, 768], P(('dp', 'tensor'))
- input_grad: bfloat16 [4096, 768], P(('dp', 'tensor'))
- qkv_weight_grad: float32 [768, 3, 768], P('dp', None, 'tensor')
- qkv_bias_grad: float32 [3, 768], replicated
- out_weight_grad: float32 [768, 768], P('tensor', 'dp')
- fc1_weight_grad: float32 [768, 3072], P('dp', 'tensor')
- fc1_bias_grad: float32 [3072], replicated
- fc2_weight_grad: float32 [3072, 768], P('tensor', 'dp')
- out_bias_grad: float32 [768], replicated
- norm1_gain_grad: float32 [768], replicated
- norm1_bias_grad: float32 [768], replicated
- norm2_gain_grad: float32 [768], replicated
- norm2_bias_grad: float32 [768], replicated
The draws below stay inside these ranges and needn't reach their ends.
Inputs may be any that keep to these rules, and one draw needn't show every extreme that they name: `segments`: each row of 512 tokens holds 4 documents of one or more tokens; a token's segment number is its document's index within the row, never falling along the row. `positions`: a token's position within its document, 0 at the document's first token.
All inputs are finite; a program needn't handle non-finite values.
Results may differ from the reference program's by a relative error of at most 0.0098.
Values may be sent and summed in bfloat16 or wider, within the bound.
A program may use at most 64 MiB of HBM per device.

```python
import math
import jax
import jax.numpy as jnp
from jax import lax

HEADS = 12
HEAD_DIM = 64
D = 768
FF = 3072
ROT = 16
LEN = 512
DOCS = 4
TOKENS = 4096


def label_rows(key):
    row_total = TOKENS // LEN

    def one_row(row_key, row_number):
        drawn = jax.random.permutation(row_key, LEN - 1)[:DOCS - 1].astype(jnp.int32) + 1
        packed = jnp.arange(1, DOCS, dtype=jnp.int32)
        cuts = jnp.where(row_number == 0, packed, drawn)
        indices = jnp.arange(LEN, dtype=jnp.int32)
        after = indices[:, None] >= cuts[None, :]
        segment_ids = jnp.sum(after.astype(jnp.int32), axis=1)
        starts = jnp.max(jnp.where(after, cuts[None, :], 0), axis=1)
        return (segment_ids, indices - starts)
    row_keys = jax.random.split(key, row_total)
    segment_ids, offsets = jax.vmap(one_row)(row_keys, jnp.arange(row_total, dtype=jnp.int32))
    return (segment_ids.reshape(-1).astype(jnp.int32), offsets.reshape(-1).astype(jnp.int32))


def draw_segments(key, part):
    return label_rows(jax.random.fold_in(key, 11))[0]


def draw_positions(key, part):
    return label_rows(jax.random.fold_in(key, 11))[1]


def draw_qkv_weight(key, part):
    main_key = jax.random.fold_in(key, 0)
    weights_all = jnp.clip(jax.random.normal(main_key, (D, 3, D), jnp.float32), -6.0, 6.0) * D ** (-0.5)
    return weights_all.astype(jnp.bfloat16)


def raised(values, stream_key, source, target, shards_of, factor):
    def block_of(position):
        return (jnp.arange(values.shape[position]) // (values.shape[position] // shards_of)).reshape((-1,) + (1,) * (values.ndim - 1 - position))

    near = jax.random.permutation(stream_key, shards_of)[block_of(target)]
    second = (block_of(target) + shards_of // 2) % shards_of
    return jnp.where((block_of(source) == near) | (block_of(source) == second), factor * values, values)


def level_of(stream_key, extent, cuts, smallest, largest):
    def one(position, shards_of):
        heights = jax.random.uniform(jax.random.fold_in(jax.random.fold_in(stream_key, 6), position), (shards_of,), jnp.float32, smallest / len(cuts), largest / len(cuts))
        return jnp.repeat(jnp.exp(heights), extent[position] // shards_of).reshape((-1,) + (1,) * (len(extent) - position - 1))

    loudness = one(*cuts[0])
    for cut in cuts[1:]:
        loudness = loudness * one(*cut)
    return loudness


def bell_draw(own_key, extent, spread, bound, cuts=(), kind=jnp.bfloat16):
    entries = jax.random.normal(own_key, extent, jnp.float32) * spread
    if len(cuts) > 0:
        entries = level_of(own_key, extent, cuts, -0.22, 0.18) * entries
    return jnp.clip(entries, min=-bound, max=bound).astype(kind)


def bell_draw_with(stream_key, extent, width, most, cuts, heavy, kind=jnp.bfloat16):
    entries = width * jax.random.normal(stream_key, extent, jnp.float32)
    if cuts:
        entries = entries * level_of(stream_key, extent, cuts, -0.22, 0.18)
    return jnp.clip(raised(entries, jax.random.fold_in(stream_key, 3), *heavy), -most, most).astype(kind)


def setup_inputs(seed: int = 0) -> dict:
    key_list = jax.random.split(jax.random.key(seed), 16)
    return {
        "layer_input": bell_draw_with(key_list[0], (TOKENS, D), 1.0, 6.0, ((0, 32),), (0, 1, 32, 2.75)),
        "cotangent": bell_draw_with(key_list[1], (TOKENS, D), 1.0, 6.0, ((0, 32),), (0, 1, 32, 2.75)),
        "segments": draw_segments(jax.random.fold_in(key_list[15], 71), 0),
        "positions": draw_positions(jax.random.fold_in(key_list[15], 71), 0),
        "norm1_gain": jnp.clip(1.0 + 0.18 * jax.random.normal(key_list[4], (D,), jnp.float32), 0.1, 1.9),
        "norm1_bias": bell_draw(key_list[5], (D,), 0.3, 1.5, (), jnp.float32),
        "norm2_gain": jnp.clip(1.0 + 0.18 * jax.random.normal(key_list[6], (D,), jnp.float32), 0.1, 1.9),
        "norm2_bias": bell_draw(key_list[7], (D,), 0.3, 1.5, (), jnp.float32),
        "qkv_weight": draw_qkv_weight(jax.random.fold_in(key_list[15], 71), 0),
        "qkv_bias": bell_draw(key_list[9], (3, D), 0.5, 2.5, ((1, 4),), jnp.float32),
        "out_weight": bell_draw(key_list[10], (D, D), (D // 16) ** -0.5, 0.875, ((0, 4), (1, 8))),
        "fc1_weight": bell_draw(key_list[11], (D, FF), D ** -0.5, 0.21875, ((0, 8), (1, 4))),
        "fc1_bias": bell_draw(key_list[12], (FF,), 0.5, 2.5, ((0, 4),), jnp.float32),
        "fc2_weight": bell_draw(key_list[13], (FF, D), FF ** -0.5, 0.109375, ((0, 4), (1, 8))),
        "out_bias": bell_draw(key_list[14], (D,), 0.5, 2.5, (), jnp.float32),
    }


EPSILON = 1e-05
NEGATIVE = -1e+30

def rotary_tables(positions):
    halves = ROT // 2
    exponent = jnp.arange(halves, dtype=jnp.float32) * (2.0 / ROT)
    freqs = jnp.power(jnp.float32(10000.0), -exponent)
    angle = positions.astype(jnp.float32)[:, None] * freqs[None, :]
    return (jnp.cos(angle)[:, None, :], jnp.sin(angle)[:, None, :])

def rotate(tensor, cosine, sine, direction):
    halves = cosine.shape[-1]
    first_half = tensor[..., :halves]
    second_half = tensor[..., halves:2 * halves]
    others = tensor[..., 2 * halves:]
    return jnp.concatenate([first_half * cosine - direction * second_half * sine, second_half * cosine + direction * first_half * sine, others], axis=-1)

def block_mask(segments, first_row, block_rows, length):
    row_ids = first_row + jnp.arange(block_rows, dtype=jnp.int32)
    col_ids = jnp.arange(length, dtype=jnp.int32)
    row_segs = lax.dynamic_slice_in_dim(segments, first_row, block_rows, 0)
    return (col_ids[None, :] <= row_ids[:, None]) & (row_segs[:, None] == segments[None, :])

def block_scores(query_block, key_rows, allowed, scale):
    scores = jnp.einsum('qhd,khd->hqk', query_block.astype(jnp.float32), key_rows.astype(jnp.float32)) * scale
    return jnp.where(allowed[None], scores, NEGATIVE)

def attention_forward(query_rows, key_rows, value_rows, segments):
    length, heads_here, head_dim = query_rows.shape
    block_rows = min(512, length)
    scale = 1.0 / math.sqrt(head_dim)
    value_float = value_rows.astype(jnp.float32)

    def one_block(block):
        first_row = (block * block_rows).astype(jnp.int32)
        query_block = lax.dynamic_slice_in_dim(query_rows, first_row, block_rows, 0)
        scores = block_scores(query_block, key_rows, block_mask(segments, first_row, block_rows, length), scale)
        peak = lax.optimization_barrier(jnp.max(scores, axis=-1, keepdims=True))
        logsum = peak[..., 0] + jnp.log(lax.optimization_barrier(jnp.sum(jnp.exp(scores - peak), axis=-1)))
        weights_low = jnp.exp(scores - logsum[..., None]).astype(jnp.bfloat16)
        output = jnp.einsum('hqk,khd->qhd', weights_low.astype(jnp.float32), value_float)
        return (output, logsum.T)
    outputs, logsums = lax.map(one_block, jnp.arange(length // block_rows, dtype=jnp.int32))
    return (outputs.reshape(length, heads_here, head_dim), logsums.reshape(length, heads_here))

def attention_backward(query_rows, key_rows, value_rows, segments, output_rows, grad_rows, logsums):
    length, heads_here, head_dim = query_rows.shape
    block_rows = min(512, length)
    scale = 1.0 / math.sqrt(head_dim)
    delta = lax.optimization_barrier(jnp.sum(grad_rows.astype(jnp.float32) * output_rows.astype(jnp.float32), axis=-1))
    key_float = key_rows.astype(jnp.float32)
    value_float = value_rows.astype(jnp.float32)

    def one_block(totals, block):
        key_grad, value_grad = totals
        first_row = (block * block_rows).astype(jnp.int32)
        query_block = lax.dynamic_slice_in_dim(query_rows, first_row, block_rows, 0)
        grad_block = lax.dynamic_slice_in_dim(grad_rows, first_row, block_rows, 0).astype(jnp.float32)
        delta_block = lax.dynamic_slice_in_dim(delta, first_row, block_rows, 0)
        logsum_block = lax.dynamic_slice_in_dim(logsums, first_row, block_rows, 0)
        scores = block_scores(query_block, key_rows, block_mask(segments, first_row, block_rows, length), scale)
        probs = jnp.exp(scores - logsum_block.T[..., None])
        probs_low = probs.astype(jnp.bfloat16)
        value_grad = value_grad + jnp.einsum('hqk,qhd->khd', probs_low.astype(jnp.float32), grad_block)
        prob_grad = jnp.einsum('qhd,khd->hqk', grad_block, value_float)
        score_low = (probs * (prob_grad - delta_block.T[..., None]) * scale).astype(jnp.bfloat16)
        score_float = score_low.astype(jnp.float32)
        query_grad = jnp.einsum('hqk,khd->qhd', score_float, key_float)
        key_grad = key_grad + jnp.einsum('hqk,qhd->khd', score_float, query_block.astype(jnp.float32))
        return ((key_grad, value_grad), query_grad)
    zeros_rows = jnp.zeros((length, heads_here, head_dim), jnp.float32)
    (key_grad, value_grad), query_grads = lax.scan(one_block, (zeros_rows, zeros_rows), jnp.arange(length // block_rows, dtype=jnp.int32))
    return (query_grads.reshape(length, heads_here, head_dim), key_grad, value_grad)

def layer_row(input_row, grad_row, segment_row, position_row, norm1_gain, norm1_bias, norm2_gain, norm2_bias, qkv_weight, qkv_bias, out_weight, fc1_weight, fc1_bias, fc2_weight, out_bias):
    length = input_row.shape[0]
    input_float = input_row.astype(jnp.float32)
    center = input_float - lax.optimization_barrier(jnp.mean(input_float, axis=-1, keepdims=True))
    inv_std = lax.rsqrt(lax.optimization_barrier(jnp.mean(center * center, axis=-1, keepdims=True)) + EPSILON)
    normed = center * inv_std
    first_in = (normed * norm1_gain + norm1_bias).astype(jnp.bfloat16)
    second_in = (normed * norm2_gain + norm2_bias).astype(jnp.bfloat16)
    qkv_matrix = qkv_weight.reshape(D, 3 * D)
    projected = jnp.dot(first_in, qkv_matrix, preferred_element_type=jnp.float32) + qkv_bias.reshape(3 * D)
    projected = projected.reshape(length, 3, HEADS, HEAD_DIM)
    cosine, sine = rotary_tables(position_row)
    query_rows = rotate(projected[:, 0], cosine, sine, 1.0).astype(jnp.bfloat16)
    key_rows = rotate(projected[:, 1], cosine, sine, 1.0).astype(jnp.bfloat16)
    value_rows = projected[:, 2].astype(jnp.bfloat16)
    attended, logsums = attention_forward(query_rows, key_rows, value_rows, segment_row)
    attended_low = attended.astype(jnp.bfloat16)
    attended_flat = attended_low.reshape(length, D)
    pre_act = jnp.dot(second_in, fc1_weight, preferred_element_type=jnp.float32) + fc1_bias
    normal_cdf = 0.5 * (1.0 + lax.erf(pre_act * (1.0 / math.sqrt(2.0))))
    hidden_low = (pre_act * normal_cdf).astype(jnp.bfloat16)
    activation_row = (input_float + jnp.dot(attended_flat, out_weight, preferred_element_type=jnp.float32) + jnp.dot(hidden_low, fc2_weight, preferred_element_type=jnp.float32) + out_bias).astype(jnp.bfloat16)
    grad_float = grad_row.astype(jnp.float32)
    hidden_grad = jnp.dot(grad_row, fc2_weight.T, preferred_element_type=jnp.float32)
    density = jnp.exp(-0.5 * pre_act * pre_act) * (1.0 / math.sqrt(2.0 * math.pi))
    pre_grad = hidden_grad * (normal_cdf + pre_act * density)
    pre_low = pre_grad.astype(jnp.bfloat16)
    fc2_grad = jnp.dot(hidden_low.T, grad_row, preferred_element_type=jnp.float32)
    fc1_grad = jnp.dot(second_in.T, pre_low, preferred_element_type=jnp.float32)
    fc1_bias_grad = lax.optimization_barrier(jnp.sum(pre_grad, axis=0))
    second_grad = jnp.dot(pre_low, fc1_weight.T, preferred_element_type=jnp.float32)
    attended_grad = jnp.dot(grad_row, out_weight.T, preferred_element_type=jnp.float32).astype(jnp.bfloat16)
    out_grad = jnp.dot(attended_flat.T, grad_row, preferred_element_type=jnp.float32)
    query_grad, key_grad, value_grad = attention_backward(query_rows, key_rows, value_rows, segment_row, attended_low, attended_grad.reshape(length, HEADS, HEAD_DIM), logsums)
    query_grad = rotate(query_grad, cosine, sine, -1.0)
    key_grad = rotate(key_grad, cosine, sine, -1.0)
    qkv_grad = jnp.stack([query_grad, key_grad, value_grad], axis=1).reshape(length, 3 * D)
    qkv_bias_grad = lax.optimization_barrier(jnp.sum(qkv_grad, axis=0)).reshape(3, D)
    qkv_low = qkv_grad.astype(jnp.bfloat16)
    qkv_weight_grad = jnp.dot(first_in.T, qkv_low, preferred_element_type=jnp.float32).reshape(D, 3, D)
    first_grad = jnp.dot(qkv_low, qkv_matrix.T, preferred_element_type=jnp.float32)
    gain1_grad = lax.optimization_barrier(jnp.sum(first_grad * normed, axis=0))
    bias1_grad = lax.optimization_barrier(jnp.sum(first_grad, axis=0))
    gain2_grad = lax.optimization_barrier(jnp.sum(second_grad * normed, axis=0))
    bias2_grad = lax.optimization_barrier(jnp.sum(second_grad, axis=0))
    out_bias_grad = lax.optimization_barrier(jnp.sum(grad_float, axis=0))
    normed_grad = first_grad * norm1_gain + second_grad * norm2_gain
    row_mean = lax.optimization_barrier(jnp.mean(normed_grad, axis=-1, keepdims=True))
    row_cross = lax.optimization_barrier(jnp.mean(normed_grad * normed, axis=-1, keepdims=True))
    input_result = (grad_float + inv_std * (normed_grad - row_mean - normed * row_cross)).astype(jnp.bfloat16)
    grads = (qkv_weight_grad, qkv_bias_grad, out_grad, fc1_grad, fc1_bias_grad, fc2_grad, out_bias_grad, gain1_grad, bias1_grad, gain2_grad, bias2_grad)
    return (activation_row, input_result, grads)

def reference(layer_input, cotangent, segments, positions, norm1_gain, norm1_bias, norm2_gain, norm2_bias, qkv_weight, qkv_bias, out_weight, fc1_weight, fc1_bias, fc2_weight, out_bias):
    row_total = layer_input.shape[0] // LEN
    input_rows = layer_input.reshape(row_total, LEN, D)
    grad_rows = cotangent.reshape(row_total, LEN, D)
    segment_rows = segments.reshape(row_total, LEN)
    position_rows = positions.reshape(row_total, LEN)

    def one_row(totals, inputs):
        input_row, grad_row, segment_row, position_row = inputs
        activation_row, input_result, grads = layer_row(input_row, grad_row, segment_row, position_row, norm1_gain, norm1_bias, norm2_gain, norm2_bias, qkv_weight, qkv_bias, out_weight, fc1_weight, fc1_bias, fc2_weight, out_bias)
        return (tuple((left + right for left, right in zip(totals, grads))), (activation_row, input_result))
    initial = (jnp.zeros((D, 3, D), jnp.float32), jnp.zeros((3, D), jnp.float32), jnp.zeros((D, D), jnp.float32), jnp.zeros((D, FF), jnp.float32), jnp.zeros((FF,), jnp.float32), jnp.zeros((FF, D), jnp.float32), jnp.zeros((D,), jnp.float32), jnp.zeros((D,), jnp.float32), jnp.zeros((D,), jnp.float32), jnp.zeros((D,), jnp.float32), jnp.zeros((D,), jnp.float32))
    totals, (activation_rows, result_rows) = lax.scan(one_row, initial, (input_rows, grad_rows, segment_rows, position_rows))
    return (activation_rows.reshape(row_total * LEN, D), result_rows.reshape(row_total * LEN, D), totals[0], totals[1], totals[2], totals[3], totals[4], totals[5], totals[6], totals[7], totals[8], totals[9], totals[10])
```

```python
import math

import functools

import jax
import jax.numpy as jnp
from jax import lax
from jax.experimental import pallas as pl
from jax.experimental.pallas import tpu as pltpu
from jax.sharding import PartitionSpec as P

HEAD_DIM = 64
FF = 3072
ROT = 16


EPSILON = 1e-05
NEGATIVE = -1e30


def layer_stats(rows_low):
    floats = rows_low.astype(jnp.float32)
    center = floats - jnp.mean(floats, axis=-1, keepdims=True)
    inv_std = lax.rsqrt(jnp.mean(center * center, axis=-1, keepdims=True) + EPSILON)
    return (center * inv_std, inv_std)


def contract_rows(left, right):
    return lax.dot_general(
        left, right, (((0,), (0,)), ((), ())), preferred_element_type=jnp.float32
    )


def contract_cols(left, right):
    return lax.dot_general(
        left, right, (((1,), (1,)), ((), ())), preferred_element_type=jnp.float32
    )


def rotary_tables(positions):
    halves = ROT // 2
    exponent = jnp.arange(halves, dtype=jnp.float32) * (2.0 / ROT)
    freqs = jnp.power(jnp.float32(10000.0), -exponent)
    angle = positions.astype(jnp.float32)[:, None] * freqs[None, :]
    return (jnp.cos(angle)[:, None, :], jnp.sin(angle)[:, None, :])


def rotate(tensor, cosine, sine, direction):
    halves = cosine.shape[-1]
    first_half = tensor[..., :halves]
    second_half = tensor[..., halves : 2 * halves]
    others = tensor[..., 2 * halves :]
    return jnp.concatenate(
        [
            first_half * cosine - direction * second_half * sine,
            second_half * cosine + direction * first_half * sine,
            others,
        ],
        axis=-1,
    )


def block_mask(segments, first_row, block_rows, length):
    row_ids = first_row + jnp.arange(block_rows, dtype=jnp.int32)
    col_ids = jnp.arange(length, dtype=jnp.int32)
    return (col_ids[None, :] <= row_ids[:, None]) & (segments[:, None] == segments[None, :])


def block_scores(query_block, key_rows, allowed, scale):
    scores = (
        jnp.einsum("qhd,khd->hqk", query_block, key_rows, preferred_element_type=jnp.float32)
        * scale
    )
    return jnp.where(allowed[None], scores, NEGATIVE)


def attention_forward(query_rows, key_rows, value_rows, segments):
    length, heads_here, head_dim = query_rows.shape
    block_rows = min(512, length)
    scale = 1.0 / math.sqrt(head_dim)

    def one_block(block):
        first_row = block * block_rows
        scores = block_scores(
            query_rows, key_rows, block_mask(segments, first_row, block_rows, length), scale
        )
        peak = jnp.max(scores, axis=-1, keepdims=True)
        logsum = peak[..., 0] + jnp.log(jnp.sum(jnp.exp(scores - peak), axis=-1))
        weights_low = jnp.exp(scores - logsum[..., None]).astype(jnp.bfloat16)
        output = jnp.einsum(
            "hqk,khd->qhd", weights_low, value_rows, preferred_element_type=jnp.float32
        )
        return (output, logsum.T)

    outputs, logsums = lax.map(one_block, jnp.arange(length // block_rows, dtype=jnp.int32))
    return (outputs.reshape(length, heads_here, head_dim), logsums.reshape(length, heads_here))


def attention_backward(query_rows, key_rows, value_rows, segments, output_rows, grad_rows, logsums):
    length, heads_here, head_dim = query_rows.shape
    block_rows = min(512, length)
    scale = 1.0 / math.sqrt(head_dim)
    delta = jnp.sum(grad_rows.astype(jnp.float32) * output_rows.astype(jnp.float32), axis=-1)

    def one_block(totals, block):
        key_grad, value_grad = totals
        first_row = block * block_rows
        scores = block_scores(
            query_rows, key_rows, block_mask(segments, first_row, block_rows, length), scale
        )
        probs = jnp.exp(scores - logsums.T[..., None])
        probs_low = probs.astype(jnp.bfloat16)
        value_grad = value_grad + jnp.einsum(
            "hqk,qhd->khd", probs_low, grad_rows, preferred_element_type=jnp.float32
        )
        prob_grad = jnp.einsum(
            "qhd,khd->hqk", grad_rows, value_rows, preferred_element_type=jnp.float32
        )
        score_low = (probs * (prob_grad - delta.T[..., None]) * scale).astype(jnp.bfloat16)
        query_grad = jnp.einsum(
            "hqk,khd->qhd", score_low, key_rows, preferred_element_type=jnp.float32
        )
        key_grad = key_grad + jnp.einsum(
            "hqk,qhd->khd", score_low, query_rows, preferred_element_type=jnp.float32
        )
        return ((key_grad, value_grad), query_grad)

    zeros_rows = jnp.zeros((length, heads_here, head_dim), jnp.float32)
    (key_grad, value_grad), query_grads = lax.scan(
        one_block, (zeros_rows, zeros_rows), jnp.arange(length // block_rows, dtype=jnp.int32)
    )
    return (query_grads.reshape(length, heads_here, head_dim), key_grad, value_grad)


def plain_body(
    layer_input,
    cotangent,
    segments,
    positions,
    norm1_gain,
    norm1_bias,
    norm2_gain,
    norm2_bias,
    qkv_weight,
    qkv_bias,
    out_weight,
    fc1_weight,
    fc1_bias,
    fc2_weight,
    out_bias,
):
    part_index = lax.axis_index("tensor")
    local_rows, width = layer_input.shape
    length = segments.shape[0]
    normed, inv_std = layer_stats(layer_input)
    first_low = (normed * norm1_gain + norm1_bias).astype(jnp.bfloat16)
    second_low = (normed * norm2_gain + norm2_bias).astype(jnp.bfloat16)
    first_in, second_in, grad_full = (
        lax.all_gather(first_low, "tensor", axis=0, tiled=True),
        lax.all_gather(second_low, "tensor", axis=0, tiled=True),
        lax.all_gather(cotangent, "tensor", axis=0, tiled=True),
    )
    qkv_full, fc1_full = (
        lax.all_gather(qkv_weight, "dp", axis=0, tiled=True),
        lax.all_gather(fc1_weight, "dp", axis=0, tiled=True),
    )
    out_full, fc2_full = (
        lax.all_gather(out_weight, "dp", axis=1, tiled=True),
        lax.all_gather(fc2_weight, "dp", axis=1, tiled=True),
    )
    local_width = qkv_full.shape[2]
    heads_here = local_width // HEAD_DIM
    qkv_matrix = qkv_full.reshape(width, 3 * local_width)
    projected = jnp.dot(
        first_in, qkv_matrix, preferred_element_type=jnp.float32
    ) + qkv_bias.reshape(3 * local_width)
    projected = projected.reshape(length, 3, heads_here, HEAD_DIM)
    cosine, sine = rotary_tables(positions)
    query_rows = rotate(projected[:, 0], cosine, sine, 1.0).astype(jnp.bfloat16)
    key_rows = rotate(projected[:, 1], cosine, sine, 1.0).astype(jnp.bfloat16)
    value_rows = projected[:, 2].astype(jnp.bfloat16)
    attended, logsums = attention_forward(query_rows, key_rows, value_rows, segments)
    attended_low = attended.astype(jnp.bfloat16)
    attended_flat = attended_low.reshape(length, local_width)
    pre_act = jnp.dot(second_in, fc1_full, preferred_element_type=jnp.float32) + fc1_bias
    normal_cdf = 0.5 * (1.0 + lax.erf(pre_act * (1.0 / math.sqrt(2.0))))
    hidden_low = (pre_act * normal_cdf).astype(jnp.bfloat16)
    branch_total = lax.psum_scatter(
        jnp.dot(attended_flat, out_full, preferred_element_type=jnp.float32)
        + jnp.dot(hidden_low, fc2_full, preferred_element_type=jnp.float32),
        "tensor",
        scatter_dimension=0,
        tiled=True,
    )
    activations = (layer_input.astype(jnp.float32) + branch_total + out_bias).astype(jnp.bfloat16)
    hidden_grad = contract_cols(grad_full, fc2_full)
    density = jnp.exp(-0.5 * pre_act * pre_act) * (1.0 / math.sqrt(2.0 * math.pi))
    pre_grad = hidden_grad * (normal_cdf + pre_act * density)
    pre_low = pre_grad.astype(jnp.bfloat16)
    fc2_grad = contract_rows(hidden_low, grad_full)
    fc1_grad = contract_rows(second_in, pre_low)
    fc1_bias_part = jnp.sum(pre_grad, axis=0)
    attended_grad = contract_cols(grad_full, out_full).astype(jnp.bfloat16)
    out_grad = contract_rows(attended_flat, grad_full)
    query_grad, key_grad, value_grad = attention_backward(
        query_rows,
        key_rows,
        value_rows,
        segments,
        attended_low,
        attended_grad.reshape(length, heads_here, HEAD_DIM),
        logsums,
    )
    query_grad = rotate(query_grad, cosine, sine, -1.0)
    key_grad = rotate(key_grad, cosine, sine, -1.0)
    qkv_grad = jnp.stack([query_grad, key_grad, value_grad], axis=1).reshape(
        length, 3 * local_width
    )
    qkv_bias_part = jnp.sum(qkv_grad, axis=0).reshape(3, local_width)
    qkv_low = qkv_grad.astype(jnp.bfloat16)
    qkv_grad_full = contract_rows(first_in, qkv_low).reshape(width, 3, local_width)
    both_grads = lax.psum_scatter(
        jnp.concatenate(
            [contract_cols(qkv_low, qkv_matrix), contract_cols(pre_low, fc1_full)], axis=1
        ),
        "tensor",
        scatter_dimension=0,
        tiled=True,
    )
    first_grad = both_grads[:, :width]
    second_grad = both_grads[:, width:]
    normed_grad = first_grad * norm1_gain + second_grad * norm2_gain
    norm_sums = (
        jnp.sum(first_grad * normed, axis=0),
        jnp.sum(first_grad, axis=0),
        jnp.sum(second_grad * normed, axis=0),
        jnp.sum(second_grad, axis=0),
    )
    row_mean = jnp.mean(normed_grad, axis=-1, keepdims=True)
    row_cross = jnp.mean(normed_grad * normed, axis=-1, keepdims=True)
    input_grad = (
        cotangent.astype(jnp.float32) + inv_std * (normed_grad - row_mean - normed * row_cross)
    ).astype(jnp.bfloat16)
    qkv_bias_whole = lax.dynamic_update_slice_in_dim(
        jnp.zeros((3, width), jnp.float32), qkv_bias_part, part_index * local_width, 1
    )
    fc1_bias_whole = lax.dynamic_update_slice_in_dim(
        jnp.zeros((FF,), jnp.float32), fc1_bias_part, part_index * fc1_bias.shape[0], 0
    )
    summed = lax.psum(
        (
            qkv_bias_whole,
            fc1_bias_whole,
            jnp.sum(cotangent.astype(jnp.float32), axis=0),
            norm_sums[0],
            norm_sums[1],
            norm_sums[2],
            norm_sums[3],
        ),
        ("dp", "tensor"),
    )
    qkv_weight_grad, fc1_weight_grad = (
        lax.psum_scatter(qkv_grad_full, "dp", scatter_dimension=0, tiled=True),
        lax.psum_scatter(fc1_grad, "dp", scatter_dimension=0, tiled=True),
    )
    out_weight_grad, fc2_weight_grad = (
        lax.psum_scatter(out_grad, "dp", scatter_dimension=1, tiled=True),
        lax.psum_scatter(fc2_grad, "dp", scatter_dimension=1, tiled=True),
    )
    return (
        activations,
        input_grad,
        qkv_weight_grad,
        summed[0],
        out_weight_grad,
        fc1_weight_grad,
        summed[1],
        fc2_weight_grad,
        summed[2],
        summed[3],
        summed[4],
        summed[5],
        summed[6],
    )


MESH = pl.DeviceIdType.MESH
NEAR = 2
BF16 = jnp.bfloat16
F32 = jnp.float32


def dot_nn(left, right):
    return lax.dot_general(left, right, (((1,), (0,)), ((), ())), preferred_element_type=F32)


def block_kernel(
    ndp,
    nt,
    heads,
    x_ref,
    c_ref,
    pos_ref,
    segc_ref,
    segr_ref,
    vec_ref,
    qkvb_ref,
    fc1b_ref,
    w_ref,
    act_ref,
    ing_ref,
    gout_ref,
    sall_ref,
    xg,
    cg,
    normed,
    n1,
    n2,
    n1t,
    n2t,
    ct,
    cost,
    sint,
    bias,
    wg,
    grads,
    ry,
    sz,
    rz,
    hidden,
    prelow,
    qkv,
    qkvlow,
    attended,
    agrad,
    nacc,
    abuf,
    nbuf,
    abufr,
    nbufr,
    small,
    small_all,
    sdp,
    tok_s,
    tok_r,
    agy_s,
    agy_r,
    agz_s,
    agz_r,
    rsy_s,
    rsy_r,
    rsz_s,
    rsz_r,
    par_s,
    par_r,
    sm_s,
    sm_r,
    st_s,
    st_r,
):
    nz = ndp // NEAR
    p = lax.axis_index("dp")
    t = lax.axis_index("tensor")
    z = p // NEAR
    y = p % NEAR
    rows, width = x_ref.shape
    length = xg.shape[0]
    shard = w_ref.shape[1]
    local = heads * HEAD_DIM
    pieces = w_ref.shape[0]
    pending = []

    def at(zi, yi):
        return zi * NEAR + yi

    def send(src, dst, ssem, rsem, dp, tn):
        copy = pltpu.make_async_remote_copy(
            src_ref=src,
            dst_ref=dst,
            send_sem=ssem,
            recv_sem=rsem,
            device_id={"dp": dp, "tensor": tn},
            device_id_type=MESH,
        )
        copy.start()
        pending.append(copy)

    def arrive(dst, ssem, rsem):
        pltpu.make_async_remote_copy(
            src_ref=dst,
            dst_ref=dst,
            send_sem=ssem,
            recv_sem=rsem,
            device_id={"dp": p, "tensor": t},
            device_id_type=MESH,
        ).wait_recv()

    def wrows(owner):
        return pl.ds(pl.multiple_of(owner * shard, shard), shard)

    def trows(owner):
        return pl.ds(pl.multiple_of(owner * rows, rows), rows)

    ypeer = at(z, 1 - y)

    def up(k):
        return lax.rem(z + k, nz)

    def down(k):
        return lax.rem(z + nz - k, nz)

    barrier = pltpu.get_barrier_semaphore()
    for k in range(1, nt):
        pl.semaphore_signal(
            barrier,
            inc=1,
            device_id={"dp": p, "tensor": lax.rem(t + k, nt)},
            device_id_type=MESH,
        )
    for k in range(1, ndp):
        pl.semaphore_signal(
            barrier,
            inc=1,
            device_id={"dp": lax.rem(p + k, ndp), "tensor": t},
            device_id_type=MESH,
        )
    pl.semaphore_wait(barrier, nt - 1 + ndp - 1)

    for k in range(1, nt):
        peer = lax.rem(t + k, nt)
        send(x_ref, xg.at[trows(t)], tok_s.at[0, k], tok_r.at[0, k], p, peer)
        send(c_ref, cg.at[trows(t)], tok_s.at[1, k], tok_r.at[1, k], p, peer)
    for i in range(pieces):
        send(w_ref.at[i], wg.at[i, wrows(p)], agy_s.at[i, 0], agy_r.at[i, 0], ypeer, t)
        for k in range(1, nz):
            send(
                w_ref.at[i],
                wg.at[i, wrows(p)],
                agz_s.at[i, k],
                agz_r.at[i, k],
                at(up(k), y),
                t,
            )

    xg[trows(t), :] = x_ref[...]
    cg[trows(t), :] = c_ref[...]
    for i in range(pieces):
        wg[i, wrows(p), :] = w_ref[i]

    halves = ROT // 2
    feature = lax.broadcasted_iota(jnp.int32, (1, HEAD_DIM), 1)
    spun = feature < ROT
    exponent = (feature % halves).astype(F32) * (2.0 / ROT)
    freqs = jnp.exp(exponent * (-math.log(10000.0)))
    angle = jnp.where(spun, pos_ref[...].astype(F32) * freqs, 0.0)
    cost[...] = jnp.cos(angle)
    sint[...] = jnp.where(feature < halves, -jnp.sin(angle), jnp.sin(angle))
    row_ids = lax.broadcasted_iota(jnp.int32, (length, length), 0)
    col_ids = lax.broadcasted_iota(jnp.int32, (length, length), 1)
    allowed = (col_ids <= row_ids) & (segc_ref[...] == segr_ref[...])
    bias[...] = jnp.where(allowed, 0.0, NEGATIVE)

    for k in range(1, nt):
        owner = lax.rem(t + nt - k, nt)
        arrive(xg.at[trows(owner)], tok_s.at[0, k], tok_r.at[0, k])
        arrive(cg.at[trows(owner)], tok_s.at[1, k], tok_r.at[1, k])

    gain1, bias1, gain2, bias2 = (vec_ref[i : i + 1, :] for i in range(4))
    for b in range(nt):
        block = slice(b * rows, (b + 1) * rows)
        value, _ = layer_stats(xg[block, :])
        normed[block, :] = value
        first = (value * gain1 + bias1).astype(BF16)
        second = (value * gain2 + bias2).astype(BF16)
        n1[block, :] = first
        n2[block, :] = second
        n1t[:, block] = first.T
        n2t[:, block] = second.T
        ct[:, block] = cg[block, :].T

    def relay(i):
        for k in range(1, nz):
            owner = at(down(k), y)
            place = wg.at[i, wrows(owner)]
            arrive(place, agz_s.at[i, k], agz_r.at[i, k])
            send(place, place, agy_s.at[i, k], agy_r.at[i, k], ypeer, t)

    def landed(i):
        for k in range(nz):
            owner = at(down(k), 1 - y)
            arrive(wg.at[i, wrows(owner)], agy_s.at[i, k], agy_r.at[i, k])

    def spread(i):
        for k in list(range(1, nz)) + [0]:
            send(
                grads.at[i, wrows(at(up(k), 1 - y))],
                ry.at[i, k],
                rsy_s.at[i, k],
                rsy_r.at[i, k],
                ypeer,
                t,
            )

    def combine(i, k):
        arrive(ry.at[i, k], rsy_s.at[i, k], rsy_r.at[i, k])
        mine = grads[i, wrows(at(up(k), y)), :].astype(F32)
        return mine + ry[i, k].astype(F32)

    def pass_on(i):
        for k in range(1, nz):
            sz[i, k] = combine(i, k).astype(BF16)
            send(
                sz.at[i, k], rz.at[i, k], rsz_s.at[i, k], rsz_r.at[i, k], at(up(k), y), t
            )

    def finish(i):
        total = combine(i, 0)
        for k in range(1, nz):
            arrive(rz.at[i, k], rsz_s.at[i, k], rsz_r.at[i, k])
            total = total + rz[i, k].astype(F32)
        gout_ref[i] = total

    relay(0)
    relay(1)
    landed(0)
    landed(1)

    ffn = fc1b_ref.shape[1]
    step = 256 if ffn % 256 == 0 else ffn
    small[...] = jnp.zeros_like(small)

    @pl.loop(0, ffn // step)
    def _(j):
        cols = pl.ds(pl.multiple_of(j * step, step), step)
        pre = dot_nn(n2[...], wg[0, :, cols]) + fc1b_ref[:, cols]
        cdf = 0.5 * (1.0 + lax.erf(pre * (1.0 / math.sqrt(2.0))))
        hidden[:, cols] = (pre * cdf).astype(BF16)
        density = jnp.exp(-0.5 * pre * pre) * (1.0 / math.sqrt(2.0 * math.pi))
        pre_grad = dot_nn(cg[...], wg[1, :, cols]) * (cdf + pre * density)
        prelow[:, cols] = pre_grad.astype(BF16)
        small[0:1, cols] = jnp.sum(pre_grad, axis=0, keepdims=True)

    relay(2)
    gstep = 256 if width % 256 == 0 else width

    @pl.loop(0, width // gstep)
    def _(j):
        part = pl.ds(pl.multiple_of(j * gstep, gstep), gstep)
        grads[0, part, :] = dot_nn(n2t[part, :], prelow[...]).astype(BF16)

    spread(0)

    @pl.loop(0, width // gstep)
    def _(j):
        part = pl.ds(pl.multiple_of(j * gstep, gstep), gstep)
        grads[1, part, :] = dot_nn(ct[part, :], hidden[...]).astype(BF16)

    spread(1)

    @pl.loop(0, nt)
    def _(b):
        part = pl.ds(pl.multiple_of(b * rows, rows), rows)
        second_grad = contract_cols(prelow[part, :], wg[0])
        small[4:5, :] += jnp.sum(second_grad * normed[part, :], axis=0, keepdims=True)
        small[5:6, :] += jnp.sum(second_grad, axis=0, keepdims=True)
        small[6:7, :] += jnp.sum(cg[part, :].astype(F32), axis=0, keepdims=True)
        nacc[part, :] = second_grad * gain2

    landed(2)
    wide = 3 * local
    qkv[...] = dot_nn(n1[...], wg[2, :, :wide]) + qkvb_ref[...]
    agrad[...] = dot_nn(cg[...], wg[2, :, wide:]).astype(BF16)
    pass_on(0)

    def swap(tensor):
        return jnp.concatenate(
            [tensor[:, halves:ROT], tensor[:, :halves], tensor[:, ROT:]], axis=1
        )

    scale = 1.0 / math.sqrt(HEAD_DIM)
    for h in range(heads):
        spots = [slice(s * local + h * HEAD_DIM, s * local + (h + 1) * HEAD_DIM) for s in range(3)]
        spot = slice(h * HEAD_DIM, (h + 1) * HEAD_DIM)
        raw_q, raw_k = qkv[:, spots[0]], qkv[:, spots[1]]
        query = (raw_q * cost[...] + swap(raw_q) * sint[...]).astype(BF16)
        key = (raw_k * cost[...] + swap(raw_k) * sint[...]).astype(BF16)
        value = qkv[:, spots[2]].astype(BF16)
        scores = contract_cols(query, key) * scale + bias[...]
        peak = jnp.max(scores, axis=-1, keepdims=True)
        powers = jnp.exp(scores - peak)
        probs = powers * (1.0 / jnp.sum(powers, axis=-1, keepdims=True))
        probs_low = probs.astype(BF16)
        out = dot_nn(probs_low, value).astype(BF16)
        attended[:, spot] = out
        grad = agrad[:, spot]
        delta = jnp.sum(grad.astype(F32) * out.astype(F32), axis=-1, keepdims=True)
        value_grad = contract_rows(probs_low, grad)
        score_low = (probs * (contract_cols(grad, value) - delta) * scale).astype(BF16)
        query_grad = dot_nn(score_low, key)
        key_grad = contract_rows(score_low, query)
        query_grad = query_grad * cost[...] - swap(query_grad) * sint[...]
        key_grad = key_grad * cost[...] - swap(key_grad) * sint[...]
        for s, g in enumerate((query_grad, key_grad, value_grad)):
            small[1:2, spots[s]] = jnp.sum(g, axis=0, keepdims=True)
            qkvlow[:, spots[s]] = g.astype(BF16)
        if h == heads // 2:
            pass_on(1)

    @pl.loop(0, width // gstep)
    def _(j):
        part = pl.ds(pl.multiple_of(j * gstep, gstep), gstep)
        grads[2, part, :wide] = dot_nn(n1t[part, :], qkvlow[...]).astype(BF16)
        grads[2, part, wide:] = dot_nn(ct[part, :], attended[...]).astype(BF16)

    spread(2)

    @pl.loop(0, nt)
    def _(b):
        part = pl.ds(pl.multiple_of(b * rows, rows), rows)
        first_grad = contract_cols(qkvlow[part, :], wg[2, :, :wide])
        small[2:3, :] += jnp.sum(first_grad * normed[part, :], axis=0, keepdims=True)
        small[3:4, :] += jnp.sum(first_grad, axis=0, keepdims=True)
        nbuf[part, :] = (nacc[part, :] + first_grad * gain1).astype(BF16)

    for k in range(1, nt):
        peer = lax.rem(t + k, nt)
        send(nbuf.at[trows(peer)], nbufr.at[k], par_s.at[1, k], par_r.at[1, k], p, peer)
    small_all[p] = small[...]
    for k in range(1, ndp):
        send(
            small, small_all.at[p], sm_s.at[k], sm_r.at[k], lax.rem(p + k, ndp), t
        )

    pass_on(2)

    @pl.loop(0, nt)
    def _(b):
        part = pl.ds(pl.multiple_of(b * rows, rows), rows)
        abuf[part, :] = (
            contract_cols(attended[part, :], wg[2, :, wide:])
            + contract_cols(hidden[part, :], wg[1])
        ).astype(BF16)

    for k in range(1, nt):
        peer = lax.rem(t + k, nt)
        send(abuf.at[trows(peer)], abufr.at[k], par_s.at[0, k], par_r.at[0, k], p, peer)

    for k in range(1, ndp):
        owner = lax.rem(p + ndp - k, ndp)
        arrive(small_all.at[owner], sm_s.at[k], sm_r.at[k])
    total = small_all[0]
    for i in range(1, ndp):
        total = total + small_all[i]
    sdp[...] = total
    sall_ref[t] = total
    for k in range(1, nt):
        peer = lax.rem(t + k, nt)
        send(sdp, sall_ref.at[t], st_s.at[k], st_r.at[k], p, peer)

    finish(0)
    finish(1)

    grad_sum = nbuf[trows(t), :].astype(F32)
    for k in range(1, nt):
        arrive(nbufr.at[k], par_s.at[1, k], par_r.at[1, k])
        grad_sum = grad_sum + nbufr[k].astype(F32)
    value, inv_std = layer_stats(x_ref[...])
    row_mean = jnp.mean(grad_sum, axis=-1, keepdims=True)
    row_cross = jnp.mean(grad_sum * value, axis=-1, keepdims=True)
    ing_ref[...] = (
        c_ref[...].astype(F32) + inv_std * (grad_sum - row_mean - value * row_cross)
    ).astype(BF16)

    branch = abuf[trows(t), :].astype(F32)
    for k in range(1, nt):
        arrive(abufr.at[k], par_s.at[0, k], par_r.at[0, k])
        branch = branch + abufr[k].astype(F32)
    act_ref[...] = (x_ref[...].astype(F32) + branch + vec_ref[4:5, :]).astype(BF16)

    for k in range(1, nt):
        owner = lax.rem(t + nt - k, nt)
        arrive(sall_ref.at[owner], st_s.at[k], st_r.at[k])
    finish(2)
    for copy in pending:
        copy.wait_send()


def body(ndp, nt, *arrays):
    (
        layer_input,
        cotangent,
        segments,
        positions,
        norm1_gain,
        norm1_bias,
        norm2_gain,
        norm2_bias,
        qkv_weight,
        qkv_bias,
        out_weight,
        fc1_weight,
        fc1_bias,
        fc2_weight,
        out_bias,
    ) = arrays
    rows, width = layer_input.shape
    length = segments.shape[0]
    shard, _, local = qkv_weight.shape
    ffn = fc1_weight.shape[1]
    heads = local // HEAD_DIM
    if ndp % NEAR or shard % 16 or rows % 128 or ffn % 128 or 4 * local != ffn or ffn != width:
        return plain_body(*arrays)
    nz = ndp // NEAR
    packed = jnp.stack(
        [
            fc1_weight,
            fc2_weight.T,
            jnp.concatenate([qkv_weight.reshape(shard, 3 * local), out_weight.T], axis=1),
        ]
    )
    vectors = jnp.stack(
        [norm1_gain, norm1_bias, norm2_gain, norm2_bias, out_bias] + [out_bias] * 3
    )
    wide = max(ffn, width)
    vm = pltpu.VMEM
    dma = pltpu.SemaphoreType.DMA
    spec = pl.BlockSpec(memory_space=pltpu.VMEM)
    act, ing, gout, sall = pl.pallas_call(
        functools.partial(block_kernel, ndp, nt, heads),
        out_shape=(
            jax.ShapeDtypeStruct((rows, width), BF16),
            jax.ShapeDtypeStruct((rows, width), BF16),
            jax.ShapeDtypeStruct((3, shard, ffn), F32),
            jax.ShapeDtypeStruct((nt, 8, wide), F32),
        ),
        in_specs=[spec] * 9,
        out_specs=(spec,) * 4,
        scratch_shapes=[
            vm((length, width), BF16),
            vm((length, width), BF16),
            vm((length, width), F32),
            vm((length, width), BF16),
            vm((length, width), BF16),
            vm((width, length), BF16),
            vm((width, length), BF16),
            vm((width, length), BF16),
            vm((length, HEAD_DIM), F32),
            vm((length, HEAD_DIM), F32),
            vm((length, length), F32),
            vm((3, width, ffn), BF16),
            vm((3, width, ffn), BF16),
            vm((3, nz, shard, ffn), BF16),
            vm((3, nz, shard, ffn), BF16),
            vm((3, nz, shard, ffn), BF16),
            vm((length, ffn), BF16),
            vm((length, ffn), BF16),
            vm((length, 3 * local), F32),
            vm((length, 3 * local), BF16),
            vm((length, local), BF16),
            vm((length, local), BF16),
            vm((length, width), F32),
            vm((length, width), BF16),
            vm((length, width), BF16),
            vm((nt, rows, width), BF16),
            vm((nt, rows, width), BF16),
            vm((8, wide), F32),
            vm((ndp, 8, wide), F32),
            vm((8, wide), F32),
            dma((2, nt)),
            dma((2, nt)),
            dma((3, nz)),
            dma((3, nz)),
            dma((3, nz)),
            dma((3, nz)),
            dma((3, nz)),
            dma((3, nz)),
            dma((3, nz)),
            dma((3, nz)),
            dma((2, nt)),
            dma((2, nt)),
            dma((ndp,)),
            dma((ndp,)),
            dma((nt,)),
            dma((nt,)),
        ],
        compiler_params=pltpu.CompilerParams(
            collective_id=0, has_side_effects=True, vmem_limit_bytes=58 * 2**20
        ),
    )(
        layer_input,
        cotangent,
        positions.reshape(length, 1),
        segments.reshape(length, 1),
        segments.reshape(1, length),
        vectors,
        qkv_bias.reshape(1, 3 * local),
        fc1_bias.reshape(1, ffn),
        packed,
    )
    qkv_bias_grad = (
        sall[:, 1, : 3 * local].reshape(nt, 3, local).transpose(1, 0, 2).reshape(3, nt * local)
    )
    sums = jnp.sum(sall[:, 2:6, :width], axis=0)
    return (
        act,
        ing,
        gout[2, :, : 3 * local].reshape(shard, 3, local),
        qkv_bias_grad,
        gout[2, :, 3 * local :].T,
        gout[0],
        sall[:, 0, :ffn].reshape(nt * ffn),
        gout[1].T,
        sall[0, 6, :width],
        sums[0],
        sums[1],
        sums[2],
        sums[3],
    )


def solution(mesh):
    return jax.shard_map(
        functools.partial(body, mesh.shape["dp"], mesh.shape["tensor"]),
        mesh=mesh,
        in_specs=(
            P(("dp", "tensor"), None),
            P(("dp", "tensor"), None),
            P("dp"),
            P("dp"),
            P(),
            P(),
            P(),
            P(),
            P("dp", None, "tensor"),
            P(None, "tensor"),
            P("tensor", "dp"),
            P("dp", "tensor"),
            P("tensor"),
            P("tensor", "dp"),
            P(),
        ),
        out_specs=(
            P(("dp", "tensor"), None),
            P(("dp", "tensor"), None),
            P("dp", None, "tensor"),
            P(),
            P("tensor", "dp"),
            P("dp", "tensor"),
            P(),
            P("tensor", "dp"),
            P(),
            P(),
            P(),
            P(),
            P(),
        ),
        check_vma=False,
    )
```

```python
import math

import functools

import jax
import jax.numpy as jnp
from jax import lax
from jax.experimental import pallas as pl
from jax.experimental.pallas import tpu as pltpu
from jax.sharding import PartitionSpec as P

HEAD_DIM = 64
FF = 3072
ROT = 16


EPSILON = 1e-05
NEGATIVE = -1e30


def layer_stats(rows_low):
    floats = rows_low.astype(jnp.float32)
    center = floats - jnp.mean(floats, axis=-1, keepdims=True)
    inv_std = lax.rsqrt(jnp.mean(center * center, axis=-1, keepdims=True) + EPSILON)
    return (center * inv_std, inv_std)


def contract_rows(left, right):
    return lax.dot_general(
        left, right, (((0,), (0,)), ((), ())), preferred_element_type=jnp.float32
    )


def contract_cols(left, right):
    return lax.dot_general(
        left, right, (((1,), (1,)), ((), ())), preferred_element_type=jnp.float32
    )


def rotary_tables(positions):
    halves = ROT // 2
    exponent = jnp.arange(halves, dtype=jnp.float32) * (2.0 / ROT)
    freqs = jnp.power(jnp.float32(10000.0), -exponent)
    angle = positions.astype(jnp.float32)[:, None] * freqs[None, :]
    return (jnp.cos(angle)[:, None, :], jnp.sin(angle)[:, None, :])


def rotate(tensor, cosine, sine, direction):
    halves = cosine.shape[-1]
    first_half = tensor[..., :halves]
    second_half = tensor[..., halves : 2 * halves]
    others = tensor[..., 2 * halves :]
    return jnp.concatenate(
        [
            first_half * cosine - direction * second_half * sine,
            second_half * cosine + direction * first_half * sine,
            others,
        ],
        axis=-1,
    )


def block_mask(segments, first_row, block_rows, length):
    row_ids = first_row + jnp.arange(block_rows, dtype=jnp.int32)
    col_ids = jnp.arange(length, dtype=jnp.int32)
    return (col_ids[None, :] <= row_ids[:, None]) & (segments[:, None] == segments[None, :])


def block_scores(query_block, key_rows, allowed, scale):
    scores = (
        jnp.einsum("qhd,khd->hqk", query_block, key_rows, preferred_element_type=jnp.float32)
        * scale
    )
    return jnp.where(allowed[None], scores, NEGATIVE)


def attention_forward(query_rows, key_rows, value_rows, segments):
    length, heads_here, head_dim = query_rows.shape
    block_rows = min(512, length)
    scale = 1.0 / math.sqrt(head_dim)

    def one_block(block):
        first_row = block * block_rows
        scores = block_scores(
            query_rows, key_rows, block_mask(segments, first_row, block_rows, length), scale
        )
        peak = jnp.max(scores, axis=-1, keepdims=True)
        logsum = peak[..., 0] + jnp.log(jnp.sum(jnp.exp(scores - peak), axis=-1))
        weights_low = jnp.exp(scores - logsum[..., None]).astype(jnp.bfloat16)
        output = jnp.einsum(
            "hqk,khd->qhd", weights_low, value_rows, preferred_element_type=jnp.float32
        )
        return (output, logsum.T)

    outputs, logsums = lax.map(one_block, jnp.arange(length // block_rows, dtype=jnp.int32))
    return (outputs.reshape(length, heads_here, head_dim), logsums.reshape(length, heads_here))


def attention_backward(query_rows, key_rows, value_rows, segments, output_rows, grad_rows, logsums):
    length, heads_here, head_dim = query_rows.shape
    block_rows = min(512, length)
    scale = 1.0 / math.sqrt(head_dim)
    delta = jnp.sum(grad_rows.astype(jnp.float32) * output_rows.astype(jnp.float32), axis=-1)

    def one_block(totals, block):
        key_grad, value_grad = totals
        first_row = block * block_rows
        scores = block_scores(
            query_rows, key_rows, block_mask(segments, first_row, block_rows, length), scale
        )
        probs = jnp.exp(scores - logsums.T[..., None])
        probs_low = probs.astype(jnp.bfloat16)
        value_grad = value_grad + jnp.einsum(
            "hqk,qhd->khd", probs_low, grad_rows, preferred_element_type=jnp.float32
        )
        prob_grad = jnp.einsum(
            "qhd,khd->hqk", grad_rows, value_rows, preferred_element_type=jnp.float32
        )
        score_low = (probs * (prob_grad - delta.T[..., None]) * scale).astype(jnp.bfloat16)
        query_grad = jnp.einsum(
            "hqk,khd->qhd", score_low, key_rows, preferred_element_type=jnp.float32
        )
        key_grad = key_grad + jnp.einsum(
            "hqk,qhd->khd", score_low, query_rows, preferred_element_type=jnp.float32
        )
        return ((key_grad, value_grad), query_grad)

    zeros_rows = jnp.zeros((length, heads_here, head_dim), jnp.float32)
    (key_grad, value_grad), query_grads = lax.scan(
        one_block, (zeros_rows, zeros_rows), jnp.arange(length // block_rows, dtype=jnp.int32)
    )
    return (query_grads.reshape(length, heads_here, head_dim), key_grad, value_grad)


def plain_body(
    layer_input,
    cotangent,
    segments,
    positions,
    norm1_gain,
    norm1_bias,
    norm2_gain,
    norm2_bias,
    qkv_weight,
    qkv_bias,
    out_weight,
    fc1_weight,
    fc1_bias,
    fc2_weight,
    out_bias,
):
    part_index = lax.axis_index("tensor")
    local_rows, width = layer_input.shape
    length = segments.shape[0]
    normed, inv_std = layer_stats(layer_input)
    first_low = (normed * norm1_gain + norm1_bias).astype(jnp.bfloat16)
    second_low = (normed * norm2_gain + norm2_bias).astype(jnp.bfloat16)
    first_in, second_in, grad_full = (
        lax.all_gather(first_low, "tensor", axis=0, tiled=True),
        lax.all_gather(second_low, "tensor", axis=0, tiled=True),
        lax.all_gather(cotangent, "tensor", axis=0, tiled=True),
    )
    qkv_full, fc1_full = (
        lax.all_gather(qkv_weight, "dp", axis=0, tiled=True),
        lax.all_gather(fc1_weight, "dp", axis=0, tiled=True),
    )
    out_full, fc2_full = (
        lax.all_gather(out_weight, "dp", axis=1, tiled=True),
        lax.all_gather(fc2_weight, "dp", axis=1, tiled=True),
    )
    local_width = qkv_full.shape[2]
    heads_here = local_width // HEAD_DIM
    qkv_matrix = qkv_full.reshape(width, 3 * local_width)
    projected = jnp.dot(
        first_in, qkv_matrix, preferred_element_type=jnp.float32
    ) + qkv_bias.reshape(3 * local_width)
    projected = projected.reshape(length, 3, heads_here, HEAD_DIM)
    cosine, sine = rotary_tables(positions)
    query_rows = rotate(projected[:, 0], cosine, sine, 1.0).astype(jnp.bfloat16)
    key_rows = rotate(projected[:, 1], cosine, sine, 1.0).astype(jnp.bfloat16)
    value_rows = projected[:, 2].astype(jnp.bfloat16)
    attended, logsums = attention_forward(query_rows, key_rows, value_rows, segments)
    attended_low = attended.astype(jnp.bfloat16)
    attended_flat = attended_low.reshape(length, local_width)
    pre_act = jnp.dot(second_in, fc1_full, preferred_element_type=jnp.float32) + fc1_bias
    normal_cdf = 0.5 * (1.0 + lax.erf(pre_act * (1.0 / math.sqrt(2.0))))
    hidden_low = (pre_act * normal_cdf).astype(jnp.bfloat16)
    branch_total = lax.psum_scatter(
        jnp.dot(attended_flat, out_full, preferred_element_type=jnp.float32)
        + jnp.dot(hidden_low, fc2_full, preferred_element_type=jnp.float32),
        "tensor",
        scatter_dimension=0,
        tiled=True,
    )
    activations = (layer_input.astype(jnp.float32) + branch_total + out_bias).astype(jnp.bfloat16)
    hidden_grad = contract_cols(grad_full, fc2_full)
    density = jnp.exp(-0.5 * pre_act * pre_act) * (1.0 / math.sqrt(2.0 * math.pi))
    pre_grad = hidden_grad * (normal_cdf + pre_act * density)
    pre_low = pre_grad.astype(jnp.bfloat16)
    fc2_grad = contract_rows(hidden_low, grad_full)
    fc1_grad = contract_rows(second_in, pre_low)
    fc1_bias_part = jnp.sum(pre_grad, axis=0)
    attended_grad = contract_cols(grad_full, out_full).astype(jnp.bfloat16)
    out_grad = contract_rows(attended_flat, grad_full)
    query_grad, key_grad, value_grad = attention_backward(
        query_rows,
        key_rows,
        value_rows,
        segments,
        attended_low,
        attended_grad.reshape(length, heads_here, HEAD_DIM),
        logsums,
    )
    query_grad = rotate(query_grad, cosine, sine, -1.0)
    key_grad = rotate(key_grad, cosine, sine, -1.0)
    qkv_grad = jnp.stack([query_grad, key_grad, value_grad], axis=1).reshape(
        length, 3 * local_width
    )
    qkv_bias_part = jnp.sum(qkv_grad, axis=0).reshape(3, local_width)
    qkv_low = qkv_grad.astype(jnp.bfloat16)
    qkv_grad_full = contract_rows(first_in, qkv_low).reshape(width, 3, local_width)
    both_grads = lax.psum_scatter(
        jnp.concatenate(
            [contract_cols(qkv_low, qkv_matrix), contract_cols(pre_low, fc1_full)], axis=1
        ),
        "tensor",
        scatter_dimension=0,
        tiled=True,
    )
    first_grad = both_grads[:, :width]
    second_grad = both_grads[:, width:]
    normed_grad = first_grad * norm1_gain + second_grad * norm2_gain
    norm_sums = (
        jnp.sum(first_grad * normed, axis=0),
        jnp.sum(first_grad, axis=0),
        jnp.sum(second_grad * normed, axis=0),
        jnp.sum(second_grad, axis=0),
    )
    row_mean = jnp.mean(normed_grad, axis=-1, keepdims=True)
    row_cross = jnp.mean(normed_grad * normed, axis=-1, keepdims=True)
    input_grad = (
        cotangent.astype(jnp.float32) + inv_std * (normed_grad - row_mean - normed * row_cross)
    ).astype(jnp.bfloat16)
    qkv_bias_whole = lax.dynamic_update_slice_in_dim(
        jnp.zeros((3, width), jnp.float32), qkv_bias_part, part_index * local_width, 1
    )
    fc1_bias_whole = lax.dynamic_update_slice_in_dim(
        jnp.zeros((FF,), jnp.float32), fc1_bias_part, part_index * fc1_bias.shape[0], 0
    )
    summed = lax.psum(
        (
            qkv_bias_whole,
            fc1_bias_whole,
            jnp.sum(cotangent.astype(jnp.float32), axis=0),
            norm_sums[0],
            norm_sums[1],
            norm_sums[2],
            norm_sums[3],
        ),
        ("dp", "tensor"),
    )
    qkv_weight_grad, fc1_weight_grad = (
        lax.psum_scatter(qkv_grad_full, "dp", scatter_dimension=0, tiled=True),
        lax.psum_scatter(fc1_grad, "dp", scatter_dimension=0, tiled=True),
    )
    out_weight_grad, fc2_weight_grad = (
        lax.psum_scatter(out_grad, "dp", scatter_dimension=1, tiled=True),
        lax.psum_scatter(fc2_grad, "dp", scatter_dimension=1, tiled=True),
    )
    return (
        activations,
        input_grad,
        qkv_weight_grad,
        summed[0],
        out_weight_grad,
        fc1_weight_grad,
        summed[1],
        fc2_weight_grad,
        summed[2],
        summed[3],
        summed[4],
        summed[5],
        summed[6],
    )


MESH = pl.DeviceIdType.MESH
NEAR = 2
BF16 = jnp.bfloat16
F32 = jnp.float32


def flat(ref):
    return ref[...].reshape(1, ref.shape[0])


def dot_nn(left, right):
    return lax.dot_general(left, right, (((1,), (0,)), ((), ())), preferred_element_type=F32)


def block_kernel(
    ndp,
    nt,
    heads,
    x_ref,
    c_ref,
    pos_ref,
    seg_ref,
    g1_ref,
    b1_ref,
    g2_ref,
    b2_ref,
    ob_ref,
    qkvb_ref,
    fc1b_ref,
    fc1_ref,
    fc2_ref,
    qkvw_ref,
    outw_ref,
    act_ref,
    ing_ref,
    gout_ref,
    sall_ref,
    xg,
    cg,
    normed,
    n1,
    n2,
    n1t,
    n2t,
    ct,
    cost,
    sint,
    bias,
    wg,
    grads,
    ry,
    sz,
    rz,
    hidden,
    slope,
    prelow,
    qkv,
    qkvlow,
    attended,
    agrad,
    nacc,
    abuf,
    nbuf,
    abufr,
    nbufr,
    small,
    small_all,
    sdp,
    wown,
    tok_s,
    tok_r,
    agy_s,
    agy_r,
    agz_s,
    agz_r,
    rsy_s,
    rsy_r,
    rsz_s,
    rsz_r,
    par_s,
    par_r,
    sm_s,
    sm_r,
    st_s,
    st_r,
):
    nz = ndp // NEAR
    p = lax.axis_index("dp")
    t = lax.axis_index("tensor")
    z = p // NEAR
    y = p % NEAR
    rows, width = x_ref.shape
    length = xg.shape[0]
    shard = fc1_ref.shape[0]
    local = heads * HEAD_DIM
    sources = (fc1_ref, fc2_ref, wown)
    pending = []

    def at(zi, yi):
        return zi * NEAR + yi

    def send(src, dst, ssem, rsem, dp, tn):
        copy = pltpu.make_async_remote_copy(
            src_ref=src,
            dst_ref=dst,
            send_sem=ssem,
            recv_sem=rsem,
            device_id={"dp": dp, "tensor": tn},
            device_id_type=MESH,
        )
        copy.start()
        pending.append(copy)

    def arrive(dst, ssem, rsem):
        pltpu.make_async_remote_copy(
            src_ref=dst,
            dst_ref=dst,
            send_sem=ssem,
            recv_sem=rsem,
            device_id={"dp": p, "tensor": t},
            device_id_type=MESH,
        ).wait_recv()

    def wrows(owner):
        return pl.ds(pl.multiple_of(owner * shard, shard), shard)

    def trows(owner):
        return pl.ds(pl.multiple_of(owner * rows, rows), rows)

    ypeer = at(z, 1 - y)

    def up(k):
        return lax.rem(z + k, nz)

    def down(k):
        return lax.rem(z + nz - k, nz)

    for i in range(3):
        wown[:, i * local : (i + 1) * local] = qkvw_ref[i]
    wown[:, 3 * local :] = outw_ref[...].T

    barrier = pltpu.get_barrier_semaphore()
    for k in range(1, nt):
        pl.semaphore_signal(
            barrier,
            inc=1,
            device_id={"dp": p, "tensor": lax.rem(t + k, nt)},
            device_id_type=MESH,
        )
    for k in range(1, ndp):
        pl.semaphore_signal(
            barrier,
            inc=1,
            device_id={"dp": lax.rem(p + k, ndp), "tensor": t},
            device_id_type=MESH,
        )
    pl.semaphore_wait(barrier, nt - 1 + ndp - 1)

    for k in range(1, nt):
        peer = lax.rem(t + k, nt)
        send(x_ref, xg.at[trows(t)], tok_s.at[0, k], tok_r.at[0, k], p, peer)
        send(c_ref, cg.at[trows(t)], tok_s.at[1, k], tok_r.at[1, k], p, peer)
    for i in (2, 0, 1):
        send(sources[i], wg.at[i, wrows(p)], agy_s.at[i, 0], agy_r.at[i, 0], ypeer, t)
        for k in range(1, nz):
            send(
                sources[i],
                wg.at[i, wrows(p)],
                agz_s.at[i, k],
                agz_r.at[i, k],
                at(up(k), y),
                t,
            )

    xg[trows(t), :] = x_ref[...]
    cg[trows(t), :] = c_ref[...]
    for i in range(3):
        wg[i, wrows(p), :] = sources[i][...]

    def column(ref):
        line = jnp.broadcast_to(flat(ref).astype(F32), (128, length))
        return line.T[:, :1]

    halves = ROT // 2
    feature = lax.broadcasted_iota(jnp.int32, (1, HEAD_DIM), 1)
    spun = feature < ROT
    exponent = (feature % halves).astype(F32) * (2.0 / ROT)
    freqs = jnp.exp(exponent * (-math.log(10000.0)))
    angle = jnp.where(spun, column(pos_ref) * freqs, 0.0)
    cost[...] = jnp.cos(angle)
    sint[...] = jnp.where(feature < halves, -jnp.sin(angle), jnp.sin(angle))
    row_ids = lax.broadcasted_iota(jnp.int32, (length, length), 0)
    col_ids = lax.broadcasted_iota(jnp.int32, (length, length), 1)
    allowed = (col_ids <= row_ids) & (column(seg_ref) == flat(seg_ref).astype(F32))
    bias[...] = jnp.where(allowed, 0.0, NEGATIVE)

    def relay(i):
        for k in range(1, nz):
            owner = at(down(k), y)
            place = wg.at[i, wrows(owner)]
            arrive(place, agz_s.at[i, k], agz_r.at[i, k])
            send(place, place, agy_s.at[i, k], agy_r.at[i, k], ypeer, t)

    def landed(i):
        for k in range(nz):
            owner = at(down(k), 1 - y)
            arrive(wg.at[i, wrows(owner)], agy_s.at[i, k], agy_r.at[i, k])

    def spread(i):
        for k in list(range(1, nz)) + [0]:
            send(
                grads.at[i, wrows(at(up(k), 1 - y))],
                ry.at[i, k],
                rsy_s.at[i, k],
                rsy_r.at[i, k],
                ypeer,
                t,
            )

    def combine(i, k):
        arrive(ry.at[i, k], rsy_s.at[i, k], rsy_r.at[i, k])
        mine = grads[i, wrows(at(up(k), y)), :].astype(F32)
        return mine + ry[i, k].astype(F32)

    def pass_on(i):
        for k in range(1, nz):
            sz[i, k] = combine(i, k).astype(BF16)
            send(
                sz.at[i, k], rz.at[i, k], rsz_s.at[i, k], rsz_r.at[i, k], at(up(k), y), t
            )

    def finish(i):
        total = combine(i, 0)
        for k in range(1, nz):
            arrive(rz.at[i, k], rsz_s.at[i, k], rsz_r.at[i, k])
            total = total + rz[i, k].astype(F32)
        gout_ref[i] = total

    gain1, bias1, gain2, bias2 = (flat(ref) for ref in (g1_ref, b1_ref, g2_ref, b2_ref))

    def norm_block(owner):
        block = trows(owner)
        value, _ = layer_stats(xg[block, :])
        normed[block, :] = value
        first = (value * gain1 + bias1).astype(BF16)
        second = (value * gain2 + bias2).astype(BF16)
        n1[block, :] = first
        n2[block, :] = second
        n1t[:, block] = first.T
        n2t[:, block] = second.T
        ct[:, block] = cg[block, :].T

    norm_block(t)
    for k in range(1, nt):
        owner = lax.rem(t + nt - k, nt)
        if k == nt - 1:
            relay(2)
        arrive(xg.at[trows(owner)], tok_s.at[0, k], tok_r.at[0, k])
        arrive(cg.at[trows(owner)], tok_s.at[1, k], tok_r.at[1, k])
        norm_block(owner)

    ffn = fc1b_ref.shape[0]
    step = 256 if ffn % 256 == 0 else ffn
    gstep = 256 if width % 256 == 0 else width
    small[...] = jnp.zeros_like(small)

    landed(2)
    wide = 3 * local
    qkv[...] = dot_nn(n1[...], wg[2, :, :wide])
    for s in range(3):
        qkv[:, s * local : (s + 1) * local] += qkvb_ref[s : s + 1, :]
    agrad[...] = dot_nn(cg[...], wg[2, :, wide:]).astype(BF16)
    def swap(tensor):
        return jnp.concatenate(
            [tensor[:, halves:ROT], tensor[:, :halves], tensor[:, ROT:]], axis=1
        )

    scale = 1.0 / math.sqrt(HEAD_DIM)
    for h in range(heads):
        spots = [slice(s * local + h * HEAD_DIM, s * local + (h + 1) * HEAD_DIM) for s in range(3)]
        spot = slice(h * HEAD_DIM, (h + 1) * HEAD_DIM)
        raw_q, raw_k = qkv[:, spots[0]], qkv[:, spots[1]]
        query = (raw_q * cost[...] + swap(raw_q) * sint[...]).astype(BF16)
        key = (raw_k * cost[...] + swap(raw_k) * sint[...]).astype(BF16)
        value = qkv[:, spots[2]].astype(BF16)
        scores = contract_cols(query, key) * scale + bias[...]
        peak = jnp.max(scores, axis=-1, keepdims=True)
        powers = jnp.exp(scores - peak)
        probs = powers * (1.0 / jnp.sum(powers, axis=-1, keepdims=True))
        probs_low = probs.astype(BF16)
        out = dot_nn(probs_low, value).astype(BF16)
        attended[:, spot] = out
        grad = agrad[:, spot]
        delta = jnp.sum(grad.astype(F32) * out.astype(F32), axis=-1, keepdims=True)
        value_grad = contract_rows(probs_low, grad)
        score_low = (probs * (contract_cols(grad, value) - delta) * scale).astype(BF16)
        query_grad = dot_nn(score_low, key)
        key_grad = contract_rows(score_low, query)
        query_grad = query_grad * cost[...] - swap(query_grad) * sint[...]
        key_grad = key_grad * cost[...] - swap(key_grad) * sint[...]
        for s, g in enumerate((query_grad, key_grad, value_grad)):
            small[1:2, spots[s]] = jnp.sum(g, axis=0, keepdims=True)
            qkvlow[:, spots[s]] = g.astype(BF16)
        if h == 0:
            relay(0)
        if h == heads - 1:
            relay(1)

    @pl.loop(0, width // gstep)
    def _(j):
        part = pl.ds(pl.multiple_of(j * gstep, gstep), gstep)
        grads[2, part, :wide] = dot_nn(n1t[part, :], qkvlow[...]).astype(BF16)
        grads[2, part, wide:] = dot_nn(ct[part, :], attended[...]).astype(BF16)

    spread(2)

    @pl.loop(0, nt)
    def _(b):
        part = pl.ds(pl.multiple_of(b * rows, rows), rows)
        first_grad = contract_cols(qkvlow[part, :], wg[2, :, :wide])
        small[2:3, :] += jnp.sum(first_grad * normed[part, :], axis=0, keepdims=True)
        small[3:4, :] += jnp.sum(first_grad, axis=0, keepdims=True)
        small[6:7, :] += jnp.sum(cg[part, :].astype(F32), axis=0, keepdims=True)
        nacc[part, :] = first_grad * gain1

    landed(0)
    small[7:8, :] = flat(fc1b_ref)

    @pl.loop(0, ffn // step)
    def _(j):
        cols = pl.ds(pl.multiple_of(j * step, step), step)
        pre = dot_nn(n2[...], wg[0, :, cols]) + small[7:8, cols]
        cdf = 0.5 * (1.0 + lax.erf(pre * (1.0 / math.sqrt(2.0))))
        hidden[:, cols] = (pre * cdf).astype(BF16)
        density = jnp.exp(-0.5 * pre * pre) * (1.0 / math.sqrt(2.0 * math.pi))
        slope[:, cols] = cdf + pre * density

    @pl.loop(0, width // gstep)
    def _(j):
        part = pl.ds(pl.multiple_of(j * gstep, gstep), gstep)
        grads[1, part, :] = dot_nn(ct[part, :], hidden[...]).astype(BF16)

    spread(1)
    pass_on(2)
    landed(1)

    @pl.loop(0, ffn // step)
    def _(j):
        cols = pl.ds(pl.multiple_of(j * step, step), step)
        pre_grad = dot_nn(cg[...], wg[1, :, cols]) * slope[:, cols]
        prelow[:, cols] = pre_grad.astype(BF16)
        small[0:1, cols] = jnp.sum(pre_grad, axis=0, keepdims=True)

    @pl.loop(0, width // gstep)
    def _(j):
        part = pl.ds(pl.multiple_of(j * gstep, gstep), gstep)
        grads[0, part, :] = dot_nn(n2t[part, :], prelow[...]).astype(BF16)

    spread(0)
    pass_on(1)

    @pl.loop(0, nt)
    def _(b):
        part = pl.ds(pl.multiple_of(b * rows, rows), rows)
        second_grad = contract_cols(prelow[part, :], wg[0])
        small[4:5, :] += jnp.sum(second_grad * normed[part, :], axis=0, keepdims=True)
        small[5:6, :] += jnp.sum(second_grad, axis=0, keepdims=True)
        nbuf[part, :] = (nacc[part, :] + second_grad * gain2).astype(BF16)

    for k in range(1, nt):
        peer = lax.rem(t + k, nt)
        send(nbuf.at[trows(peer)], nbufr.at[k], par_s.at[1, k], par_r.at[1, k], p, peer)
    small_all[p] = small[...]
    for k in range(1, ndp):
        send(
            small, small_all.at[p], sm_s.at[k], sm_r.at[k], lax.rem(p + k, ndp), t
        )

    @pl.loop(0, nt)
    def _(b):
        part = pl.ds(pl.multiple_of(b * rows, rows), rows)
        abuf[part, :] = (
            contract_cols(attended[part, :], wg[2, :, wide:])
            + contract_cols(hidden[part, :], wg[1])
        ).astype(BF16)

    for k in range(1, nt):
        peer = lax.rem(t + k, nt)
        send(abuf.at[trows(peer)], abufr.at[k], par_s.at[0, k], par_r.at[0, k], p, peer)
    finish(2)
    pass_on(0)

    for k in range(1, ndp):
        owner = lax.rem(p + ndp - k, ndp)
        arrive(small_all.at[owner], sm_s.at[k], sm_r.at[k])
    total = small_all[0]
    for i in range(1, ndp):
        total = total + small_all[i]
    sdp[...] = total
    sall_ref[t] = total
    for k in range(1, nt):
        peer = lax.rem(t + k, nt)
        send(sdp, sall_ref.at[t], st_s.at[k], st_r.at[k], p, peer)

    finish(1)

    grad_sum = nbuf[trows(t), :].astype(F32)
    for k in range(1, nt):
        arrive(nbufr.at[k], par_s.at[1, k], par_r.at[1, k])
        grad_sum = grad_sum + nbufr[k].astype(F32)
    value, inv_std = layer_stats(x_ref[...])
    row_mean = jnp.mean(grad_sum, axis=-1, keepdims=True)
    row_cross = jnp.mean(grad_sum * value, axis=-1, keepdims=True)
    ing_ref[...] = (
        c_ref[...].astype(F32) + inv_std * (grad_sum - row_mean - value * row_cross)
    ).astype(BF16)

    branch = abuf[trows(t), :].astype(F32)
    for k in range(1, nt):
        arrive(abufr.at[k], par_s.at[0, k], par_r.at[0, k])
        branch = branch + abufr[k].astype(F32)
    act_ref[...] = (x_ref[...].astype(F32) + branch + flat(ob_ref)).astype(BF16)

    for k in range(1, nt):
        owner = lax.rem(t + nt - k, nt)
        arrive(sall_ref.at[owner], st_s.at[k], st_r.at[k])
    finish(0)
    for copy in pending:
        copy.wait_send()


def output_kernel(
    act_ref,
    ing_ref,
    gout_ref,
    sall_ref,
    act_out,
    ing_out,
    qkv_out,
    qkvb_out,
    out_out,
    fc1_out,
    fc1b_out,
    fc2_out,
    outb_out,
    gain1_out,
    bias1_out,
    gain2_out,
    bias2_out,
):
    act_out[...] = act_ref[...]
    ing_out[...] = ing_ref[...]
    local = out_out.shape[0]
    ffn = fc2_out.shape[1]
    nt = sall_ref.shape[0]
    width = outb_out.shape[0]
    third = gout_ref[2]
    for s in range(3):
        qkv_out[s] = third[:, s * local : (s + 1) * local]
    out_out[...] = third[:, 3 * local :].T
    fc1_out[...] = gout_ref[0]
    fc2_out[...] = gout_ref[1]
    for i in range(nt):
        fc1b_out[i * ffn : (i + 1) * ffn] = sall_ref[i, 0:1, :ffn].reshape(ffn)
        for s in range(3):
            qkvb_out[s : s + 1, i * local : (i + 1) * local] = sall_ref[
                i, 1:2, s * local : (s + 1) * local
            ]
    sums = sall_ref[0, :, :width]
    for i in range(1, nt):
        sums = sums + sall_ref[i, :, :width]
    for row, ref in ((2, gain1_out), (3, bias1_out), (4, gain2_out), (5, bias2_out)):
        ref[...] = sums[row : row + 1, :].reshape(width)
    outb_out[...] = sall_ref[0, 6:7, :width].reshape(width)


def body(ndp, nt, *arrays):
    (
        layer_input,
        cotangent,
        segments,
        positions,
        norm1_gain,
        norm1_bias,
        norm2_gain,
        norm2_bias,
        qkv_weight,
        qkv_bias,
        out_weight,
        fc1_weight,
        fc1_bias,
        fc2_weight,
        out_bias,
    ) = arrays
    rows, width = layer_input.shape
    length = segments.shape[0]
    shard, _, local = qkv_weight.shape
    ffn = fc1_weight.shape[1]
    heads = local // HEAD_DIM
    if ndp % NEAR or shard % 16 or rows % 128 or ffn % 128 or 4 * local != ffn or ffn != width:
        return plain_body(*arrays)
    nz = ndp // NEAR
    wide = max(ffn, width)
    vm = pltpu.VMEM
    dma = pltpu.SemaphoreType.DMA
    spec = pl.BlockSpec(memory_space=pltpu.VMEM)
    act, ing, gout, sall = pl.pallas_call(
        functools.partial(block_kernel, ndp, nt, heads),
        out_shape=(
            jax.ShapeDtypeStruct((rows, width), BF16),
            jax.ShapeDtypeStruct((rows, width), BF16),
            jax.ShapeDtypeStruct((3, shard, ffn), F32),
            jax.ShapeDtypeStruct((nt, 8, wide), F32),
        ),
        in_specs=[spec] * 15,
        out_specs=(spec,) * 4,
        scratch_shapes=[
            vm((length, width), BF16),
            vm((length, width), BF16),
            vm((length, width), F32),
            vm((length, width), BF16),
            vm((length, width), BF16),
            vm((width, length), BF16),
            vm((width, length), BF16),
            vm((width, length), BF16),
            vm((length, HEAD_DIM), F32),
            vm((length, HEAD_DIM), F32),
            vm((length, length), F32),
            vm((3, width, ffn), BF16),
            vm((3, width, ffn), BF16),
            vm((3, nz, shard, ffn), BF16),
            vm((3, nz, shard, ffn), BF16),
            vm((3, nz, shard, ffn), BF16),
            vm((length, ffn), BF16),
            vm((length, ffn), F32),
            vm((length, ffn), BF16),
            vm((length, 3 * local), F32),
            vm((length, 3 * local), BF16),
            vm((length, local), BF16),
            vm((length, local), BF16),
            vm((length, width), F32),
            vm((length, width), BF16),
            vm((length, width), BF16),
            vm((nt, rows, width), BF16),
            vm((nt, rows, width), BF16),
            vm((8, wide), F32),
            vm((ndp, 8, wide), F32),
            vm((8, wide), F32),
            vm((shard, ffn), BF16),
            dma((2, nt)),
            dma((2, nt)),
            dma((3, nz)),
            dma((3, nz)),
            dma((3, nz)),
            dma((3, nz)),
            dma((3, nz)),
            dma((3, nz)),
            dma((3, nz)),
            dma((3, nz)),
            dma((2, nt)),
            dma((2, nt)),
            dma((ndp,)),
            dma((ndp,)),
            dma((nt,)),
            dma((nt,)),
        ],
        compiler_params=pltpu.CompilerParams(
            collective_id=0, has_side_effects=True, vmem_limit_bytes=58 * 2**20
        ),
    )(
        layer_input,
        cotangent,
        positions,
        segments,
        norm1_gain,
        norm1_bias,
        norm2_gain,
        norm2_bias,
        out_bias,
        qkv_bias,
        fc1_bias,
        fc1_weight,
        fc2_weight.T,
        qkv_weight.transpose(1, 0, 2),
        out_weight,
    )
    line = jax.ShapeDtypeStruct((width,), F32)
    outs = pl.pallas_call(
        output_kernel,
        out_shape=(
            jax.ShapeDtypeStruct((rows, width), BF16),
            jax.ShapeDtypeStruct((rows, width), BF16),
            jax.ShapeDtypeStruct((3, shard, local), F32),
            jax.ShapeDtypeStruct((3, nt * local), F32),
            jax.ShapeDtypeStruct((local, shard), F32),
            jax.ShapeDtypeStruct((shard, ffn), F32),
            jax.ShapeDtypeStruct((nt * ffn,), F32),
            jax.ShapeDtypeStruct((shard, ffn), F32),
        )
        + (line,) * 5,
        in_specs=[spec] * 4,
        out_specs=(spec,) * 13,
    )(act, ing, gout, sall)
    return (*outs[:2], outs[2].transpose(1, 0, 2), *outs[3:7], outs[7].T, *outs[8:])


def solution(mesh):
    return jax.shard_map(
        functools.partial(body, mesh.shape["dp"], mesh.shape["tensor"]),
        mesh=mesh,
        in_specs=(
            P(("dp", "tensor"), None),
            P(("dp", "tensor"), None),
            P("dp"),
            P("dp"),
            P(),
            P(),
            P(),
            P(),
            P("dp", None, "tensor"),
            P(None, "tensor"),
            P("tensor", "dp"),
            P("dp", "tensor"),
            P("tensor"),
            P("tensor", "dp"),
            P(),
        ),
        out_specs=(
            P(("dp", "tensor"), None),
            P(("dp", "tensor"), None),
            P("dp", None, "tensor"),
            P(),
            P("tensor", "dp"),
            P("dp", "tensor"),
            P(),
            P("tensor", "dp"),
            P(),
            P(),
            P(),
            P(),
            P(),
        ),
        check_vma=False,
    )
```

```python
import math

import functools

import jax
import jax.numpy as jnp
from jax import lax
from jax.experimental import pallas as pl
from jax.experimental.pallas import tpu as pltpu
from jax.sharding import PartitionSpec as P

HEAD_DIM = 64
FF = 3072
ROT = 16


EPSILON = 1e-05
NEGATIVE = -1e30


def layer_stats(rows_low):
    floats = rows_low.astype(jnp.float32)
    center = floats - jnp.mean(floats, axis=-1, keepdims=True)
    inv_std = lax.rsqrt(jnp.mean(center * center, axis=-1, keepdims=True) + EPSILON)
    return (center * inv_std, inv_std)


def contract_rows(left, right):
    return lax.dot_general(
        left, right, (((0,), (0,)), ((), ())), preferred_element_type=jnp.float32
    )


def contract_cols(left, right):
    return lax.dot_general(
        left, right, (((1,), (1,)), ((), ())), preferred_element_type=jnp.float32
    )


def rotary_tables(positions):
    halves = ROT // 2
    exponent = jnp.arange(halves, dtype=jnp.float32) * (2.0 / ROT)
    freqs = jnp.power(jnp.float32(10000.0), -exponent)
    angle = positions.astype(jnp.float32)[:, None] * freqs[None, :]
    return (jnp.cos(angle)[:, None, :], jnp.sin(angle)[:, None, :])


def rotate(tensor, cosine, sine, direction):
    halves = cosine.shape[-1]
    first_half = tensor[..., :halves]
    second_half = tensor[..., halves : 2 * halves]
    others = tensor[..., 2 * halves :]
    return jnp.concatenate(
        [
            first_half * cosine - direction * second_half * sine,
            second_half * cosine + direction * first_half * sine,
            others,
        ],
        axis=-1,
    )


def block_mask(segments, first_row, block_rows, length):
    row_ids = first_row + jnp.arange(block_rows, dtype=jnp.int32)
    col_ids = jnp.arange(length, dtype=jnp.int32)
    return (col_ids[None, :] <= row_ids[:, None]) & (segments[:, None] == segments[None, :])


def block_scores(query_block, key_rows, allowed, scale):
    scores = (
        jnp.einsum("qhd,khd->hqk", query_block, key_rows, preferred_element_type=jnp.float32)
        * scale
    )
    return jnp.where(allowed[None], scores, NEGATIVE)


def attention_forward(query_rows, key_rows, value_rows, segments):
    length, heads_here, head_dim = query_rows.shape
    block_rows = min(512, length)
    scale = 1.0 / math.sqrt(head_dim)

    def one_block(block):
        first_row = block * block_rows
        scores = block_scores(
            query_rows, key_rows, block_mask(segments, first_row, block_rows, length), scale
        )
        peak = jnp.max(scores, axis=-1, keepdims=True)
        logsum = peak[..., 0] + jnp.log(jnp.sum(jnp.exp(scores - peak), axis=-1))
        weights_low = jnp.exp(scores - logsum[..., None]).astype(jnp.bfloat16)
        output = jnp.einsum(
            "hqk,khd->qhd", weights_low, value_rows, preferred_element_type=jnp.float32
        )
        return (output, logsum.T)

    outputs, logsums = lax.map(one_block, jnp.arange(length // block_rows, dtype=jnp.int32))
    return (outputs.reshape(length, heads_here, head_dim), logsums.reshape(length, heads_here))


def attention_backward(query_rows, key_rows, value_rows, segments, output_rows, grad_rows, logsums):
    length, heads_here, head_dim = query_rows.shape
    block_rows = min(512, length)
    scale = 1.0 / math.sqrt(head_dim)
    delta = jnp.sum(grad_rows.astype(jnp.float32) * output_rows.astype(jnp.float32), axis=-1)

    def one_block(totals, block):
        key_grad, value_grad = totals
        first_row = block * block_rows
        scores = block_scores(
            query_rows, key_rows, block_mask(segments, first_row, block_rows, length), scale
        )
        probs = jnp.exp(scores - logsums.T[..., None])
        probs_low = probs.astype(jnp.bfloat16)
        value_grad = value_grad + jnp.einsum(
            "hqk,qhd->khd", probs_low, grad_rows, preferred_element_type=jnp.float32
        )
        prob_grad = jnp.einsum(
            "qhd,khd->hqk", grad_rows, value_rows, preferred_element_type=jnp.float32
        )
        score_low = (probs * (prob_grad - delta.T[..., None]) * scale).astype(jnp.bfloat16)
        query_grad = jnp.einsum(
            "hqk,khd->qhd", score_low, key_rows, preferred_element_type=jnp.float32
        )
        key_grad = key_grad + jnp.einsum(
            "hqk,qhd->khd", score_low, query_rows, preferred_element_type=jnp.float32
        )
        return ((key_grad, value_grad), query_grad)

    zeros_rows = jnp.zeros((length, heads_here, head_dim), jnp.float32)
    (key_grad, value_grad), query_grads = lax.scan(
        one_block, (zeros_rows, zeros_rows), jnp.arange(length // block_rows, dtype=jnp.int32)
    )
    return (query_grads.reshape(length, heads_here, head_dim), key_grad, value_grad)


def plain_body(
    layer_input,
    cotangent,
    segments,
    positions,
    norm1_gain,
    norm1_bias,
    norm2_gain,
    norm2_bias,
    qkv_weight,
    qkv_bias,
    out_weight,
    fc1_weight,
    fc1_bias,
    fc2_weight,
    out_bias,
):
    part_index = lax.axis_index("tensor")
    local_rows, width = layer_input.shape
    length = segments.shape[0]
    normed, inv_std = layer_stats(layer_input)
    first_low = (normed * norm1_gain + norm1_bias).astype(jnp.bfloat16)
    second_low = (normed * norm2_gain + norm2_bias).astype(jnp.bfloat16)
    first_in, second_in, grad_full = (
        lax.all_gather(first_low, "tensor", axis=0, tiled=True),
        lax.all_gather(second_low, "tensor", axis=0, tiled=True),
        lax.all_gather(cotangent, "tensor", axis=0, tiled=True),
    )
    qkv_full, fc1_full = (
        lax.all_gather(qkv_weight, "dp", axis=0, tiled=True),
        lax.all_gather(fc1_weight, "dp", axis=0, tiled=True),
    )
    out_full, fc2_full = (
        lax.all_gather(out_weight, "dp", axis=1, tiled=True),
        lax.all_gather(fc2_weight, "dp", axis=1, tiled=True),
    )
    local_width = qkv_full.shape[2]
    heads_here = local_width // HEAD_DIM
    qkv_matrix = qkv_full.reshape(width, 3 * local_width)
    projected = jnp.dot(
        first_in, qkv_matrix, preferred_element_type=jnp.float32
    ) + qkv_bias.reshape(3 * local_width)
    projected = projected.reshape(length, 3, heads_here, HEAD_DIM)
    cosine, sine = rotary_tables(positions)
    query_rows = rotate(projected[:, 0], cosine, sine, 1.0).astype(jnp.bfloat16)
    key_rows = rotate(projected[:, 1], cosine, sine, 1.0).astype(jnp.bfloat16)
    value_rows = projected[:, 2].astype(jnp.bfloat16)
    attended, logsums = attention_forward(query_rows, key_rows, value_rows, segments)
    attended_low = attended.astype(jnp.bfloat16)
    attended_flat = attended_low.reshape(length, local_width)
    pre_act = jnp.dot(second_in, fc1_full, preferred_element_type=jnp.float32) + fc1_bias
    normal_cdf = 0.5 * (1.0 + lax.erf(pre_act * (1.0 / math.sqrt(2.0))))
    hidden_low = (pre_act * normal_cdf).astype(jnp.bfloat16)
    branch_total = lax.psum_scatter(
        jnp.dot(attended_flat, out_full, preferred_element_type=jnp.float32)
        + jnp.dot(hidden_low, fc2_full, preferred_element_type=jnp.float32),
        "tensor",
        scatter_dimension=0,
        tiled=True,
    )
    activations = (layer_input.astype(jnp.float32) + branch_total + out_bias).astype(jnp.bfloat16)
    hidden_grad = contract_cols(grad_full, fc2_full)
    density = jnp.exp(-0.5 * pre_act * pre_act) * (1.0 / math.sqrt(2.0 * math.pi))
    pre_grad = hidden_grad * (normal_cdf + pre_act * density)
    pre_low = pre_grad.astype(jnp.bfloat16)
    fc2_grad = contract_rows(hidden_low, grad_full)
    fc1_grad = contract_rows(second_in, pre_low)
    fc1_bias_part = jnp.sum(pre_grad, axis=0)
    attended_grad = contract_cols(grad_full, out_full).astype(jnp.bfloat16)
    out_grad = contract_rows(attended_flat, grad_full)
    query_grad, key_grad, value_grad = attention_backward(
        query_rows,
        key_rows,
        value_rows,
        segments,
        attended_low,
        attended_grad.reshape(length, heads_here, HEAD_DIM),
        logsums,
    )
    query_grad = rotate(query_grad, cosine, sine, -1.0)
    key_grad = rotate(key_grad, cosine, sine, -1.0)
    qkv_grad = jnp.stack([query_grad, key_grad, value_grad], axis=1).reshape(
        length, 3 * local_width
    )
    qkv_bias_part = jnp.sum(qkv_grad, axis=0).reshape(3, local_width)
    qkv_low = qkv_grad.astype(jnp.bfloat16)
    qkv_grad_full = contract_rows(first_in, qkv_low).reshape(width, 3, local_width)
    both_grads = lax.psum_scatter(
        jnp.concatenate(
            [contract_cols(qkv_low, qkv_matrix), contract_cols(pre_low, fc1_full)], axis=1
        ),
        "tensor",
        scatter_dimension=0,
        tiled=True,
    )
    first_grad = both_grads[:, :width]
    second_grad = both_grads[:, width:]
    normed_grad = first_grad * norm1_gain + second_grad * norm2_gain
    norm_sums = (
        jnp.sum(first_grad * normed, axis=0),
        jnp.sum(first_grad, axis=0),
        jnp.sum(second_grad * normed, axis=0),
        jnp.sum(second_grad, axis=0),
    )
    row_mean = jnp.mean(normed_grad, axis=-1, keepdims=True)
    row_cross = jnp.mean(normed_grad * normed, axis=-1, keepdims=True)
    input_grad = (
        cotangent.astype(jnp.float32) + inv_std * (normed_grad - row_mean - normed * row_cross)
    ).astype(jnp.bfloat16)
    qkv_bias_whole = lax.dynamic_update_slice_in_dim(
        jnp.zeros((3, width), jnp.float32), qkv_bias_part, part_index * local_width, 1
    )
    fc1_bias_whole = lax.dynamic_update_slice_in_dim(
        jnp.zeros((FF,), jnp.float32), fc1_bias_part, part_index * fc1_bias.shape[0], 0
    )
    summed = lax.psum(
        (
            qkv_bias_whole,
            fc1_bias_whole,
            jnp.sum(cotangent.astype(jnp.float32), axis=0),
            norm_sums[0],
            norm_sums[1],
            norm_sums[2],
            norm_sums[3],
        ),
        ("dp", "tensor"),
    )
    qkv_weight_grad, fc1_weight_grad = (
        lax.psum_scatter(qkv_grad_full, "dp", scatter_dimension=0, tiled=True),
        lax.psum_scatter(fc1_grad, "dp", scatter_dimension=0, tiled=True),
    )
    out_weight_grad, fc2_weight_grad = (
        lax.psum_scatter(out_grad, "dp", scatter_dimension=1, tiled=True),
        lax.psum_scatter(fc2_grad, "dp", scatter_dimension=1, tiled=True),
    )
    return (
        activations,
        input_grad,
        qkv_weight_grad,
        summed[0],
        out_weight_grad,
        fc1_weight_grad,
        summed[1],
        fc2_weight_grad,
        summed[2],
        summed[3],
        summed[4],
        summed[5],
        summed[6],
    )


MESH = pl.DeviceIdType.MESH
NEAR = 2
BF16 = jnp.bfloat16
F32 = jnp.float32


def flat(ref):
    return ref[...].reshape(1, ref.shape[0])


def dot_nn(left, right):
    return lax.dot_general(left, right, (((1,), (0,)), ((), ())), preferred_element_type=F32)


def block_kernel(
    ndp,
    nt,
    heads,
    x_ref,
    c_ref,
    pos_ref,
    seg_ref,
    g1_ref,
    b1_ref,
    g2_ref,
    b2_ref,
    ob_ref,
    qkvb_ref,
    fc1b_ref,
    fc1_ref,
    fc2_ref,
    qkvw_ref,
    outw_ref,
    act_ref,
    ing_ref,
    gout_ref,
    sall_ref,
    xg,
    cg,
    normed,
    n1,
    n2,
    n1t,
    n2t,
    ct,
    cost,
    sint,
    bias,
    wg,
    grads,
    ry,
    sz,
    rz,
    hidden,
    slope,
    prelow,
    qkv,
    qkvlow,
    attended,
    agrad,
    nacc,
    abuf,
    nbuf,
    abufr,
    nbufr,
    small,
    small_all,
    sdp,
    wown,
    tok_s,
    tok_r,
    agy_s,
    agy_r,
    agz_s,
    agz_r,
    rsy_s,
    rsy_r,
    rsz_s,
    rsz_r,
    par_s,
    par_r,
    sm_s,
    sm_r,
    st_s,
    st_r,
):
    nz = ndp // NEAR
    p = lax.axis_index("dp")
    t = lax.axis_index("tensor")
    z = p // NEAR
    y = p % NEAR
    rows, width = x_ref.shape
    length = xg.shape[0]
    shard = fc1_ref.shape[0]
    local = heads * HEAD_DIM
    sources = (fc1_ref, fc2_ref, wown)
    pending = []

    def at(zi, yi):
        return zi * NEAR + yi

    def send(src, dst, ssem, rsem, dp, tn):
        copy = pltpu.make_async_remote_copy(
            src_ref=src,
            dst_ref=dst,
            send_sem=ssem,
            recv_sem=rsem,
            device_id={"dp": dp, "tensor": tn},
            device_id_type=MESH,
        )
        copy.start()
        pending.append(copy)

    def arrive(dst, ssem, rsem):
        pltpu.make_async_remote_copy(
            src_ref=dst,
            dst_ref=dst,
            send_sem=ssem,
            recv_sem=rsem,
            device_id={"dp": p, "tensor": t},
            device_id_type=MESH,
        ).wait_recv()

    def wrows(owner):
        return pl.ds(pl.multiple_of(owner * shard, shard), shard)

    def trows(owner):
        return pl.ds(pl.multiple_of(owner * rows, rows), rows)

    ypeer = at(z, 1 - y)

    def up(k):
        return lax.rem(z + k, nz)

    def down(k):
        return lax.rem(z + nz - k, nz)

    for i in range(3):
        wown[:, i * local : (i + 1) * local] = qkvw_ref[i]
    wown[:, 3 * local :] = outw_ref[...].T

    barrier = pltpu.get_barrier_semaphore()
    for k in range(1, nt):
        pl.semaphore_signal(
            barrier,
            inc=1,
            device_id={"dp": p, "tensor": lax.rem(t + k, nt)},
            device_id_type=MESH,
        )
    for k in range(1, ndp):
        pl.semaphore_signal(
            barrier,
            inc=1,
            device_id={"dp": lax.rem(p + k, ndp), "tensor": t},
            device_id_type=MESH,
        )
    pl.semaphore_wait(barrier, nt - 1 + ndp - 1)

    for k in range(1, nt):
        peer = lax.rem(t + k, nt)
        send(x_ref, xg.at[trows(t)], tok_s.at[0, k], tok_r.at[0, k], p, peer)
        send(c_ref, cg.at[trows(t)], tok_s.at[1, k], tok_r.at[1, k], p, peer)
    for i in (2, 0, 1):
        send(sources[i], wg.at[i, wrows(p)], agy_s.at[i, 0], agy_r.at[i, 0], ypeer, t)
        for k in range(1, nz):
            send(
                sources[i],
                wg.at[i, wrows(p)],
                agz_s.at[i, k],
                agz_r.at[i, k],
                at(up(k), y),
                t,
            )

    xg[trows(t), :] = x_ref[...]
    cg[trows(t), :] = c_ref[...]
    for i in range(3):
        wg[i, wrows(p), :] = sources[i][...]

    def column(ref):
        line = jnp.broadcast_to(flat(ref).astype(F32), (128, length))
        return line.T[:, :1]

    halves = ROT // 2
    feature = lax.broadcasted_iota(jnp.int32, (1, HEAD_DIM), 1)
    spun = feature < ROT
    exponent = (feature % halves).astype(F32) * (2.0 / ROT)
    freqs = jnp.exp(exponent * (-math.log(10000.0)))
    angle = jnp.where(spun, column(pos_ref) * freqs, 0.0)
    cost[...] = jnp.cos(angle)
    sint[...] = jnp.where(feature < halves, -jnp.sin(angle), jnp.sin(angle))
    row_ids = lax.broadcasted_iota(jnp.int32, (length, length), 0)
    col_ids = lax.broadcasted_iota(jnp.int32, (length, length), 1)
    allowed = (col_ids <= row_ids) & (column(seg_ref) == flat(seg_ref).astype(F32))
    bias[...] = jnp.where(allowed, 0.0, NEGATIVE)

    def relay(i):
        for k in range(1, nz):
            owner = at(down(k), y)
            place = wg.at[i, wrows(owner)]
            arrive(place, agz_s.at[i, k], agz_r.at[i, k])
            send(place, place, agy_s.at[i, k], agy_r.at[i, k], ypeer, t)

    def landed(i):
        for k in range(nz):
            owner = at(down(k), 1 - y)
            arrive(wg.at[i, wrows(owner)], agy_s.at[i, k], agy_r.at[i, k])

    def spread(i, terms):
        for k in list(range(1, nz)) + [0]:
            start = pl.multiple_of(up(k) * (NEAR * shard), NEAR * shard)
            part = pl.ds(start, NEAR * shard)
            for cols, left, right in terms:
                grads[i, part, cols] = dot_nn(left[part, :], right[...]).astype(BF16)
            send(
                grads.at[i, wrows(at(up(k), 1 - y))],
                ry.at[i, k],
                rsy_s.at[i, k],
                rsy_r.at[i, k],
                ypeer,
                t,
            )

    def combine(i, k):
        arrive(ry.at[i, k], rsy_s.at[i, k], rsy_r.at[i, k])
        mine = grads[i, wrows(at(up(k), y)), :].astype(F32)
        return mine + ry[i, k].astype(F32)

    def pass_on(i):
        for k in range(1, nz):
            sz[i, k] = combine(i, k).astype(BF16)
            send(
                sz.at[i, k], rz.at[i, k], rsz_s.at[i, k], rsz_r.at[i, k], at(up(k), y), t
            )

    def finish(i):
        total = combine(i, 0)
        for k in range(1, nz):
            arrive(rz.at[i, k], rsz_s.at[i, k], rsz_r.at[i, k])
            total = total + rz[i, k].astype(F32)
        gout_ref[i] = total

    gain1, bias1, gain2, bias2 = (flat(ref) for ref in (g1_ref, b1_ref, g2_ref, b2_ref))

    def norm_block(owner):
        block = trows(owner)
        value, _ = layer_stats(xg[block, :])
        normed[block, :] = value
        first = (value * gain1 + bias1).astype(BF16)
        second = (value * gain2 + bias2).astype(BF16)
        n1[block, :] = first
        n2[block, :] = second
        n1t[:, block] = first.T
        n2t[:, block] = second.T
        ct[:, block] = cg[block, :].T

    norm_block(t)
    for k in range(1, nt):
        owner = lax.rem(t + nt - k, nt)
        if k == nt - 1:
            relay(2)
        arrive(xg.at[trows(owner)], tok_s.at[0, k], tok_r.at[0, k])
        arrive(cg.at[trows(owner)], tok_s.at[1, k], tok_r.at[1, k])
        norm_block(owner)

    ffn = fc1b_ref.shape[0]
    step = 256 if ffn % 256 == 0 else ffn
    small[...] = jnp.zeros_like(small)

    landed(2)
    wide = 3 * local
    qkv[...] = dot_nn(n1[...], wg[2, :, :wide])
    for s in range(3):
        qkv[:, s * local : (s + 1) * local] += qkvb_ref[s : s + 1, :]
    agrad[...] = dot_nn(cg[...], wg[2, :, wide:]).astype(BF16)
    def swap(tensor):
        return jnp.concatenate(
            [tensor[:, halves:ROT], tensor[:, :halves], tensor[:, ROT:]], axis=1
        )

    scale = 1.0 / math.sqrt(HEAD_DIM)
    for h in range(heads):
        spots = [slice(s * local + h * HEAD_DIM, s * local + (h + 1) * HEAD_DIM) for s in range(3)]
        spot = slice(h * HEAD_DIM, (h + 1) * HEAD_DIM)
        raw_q, raw_k = qkv[:, spots[0]], qkv[:, spots[1]]
        query = (raw_q * cost[...] + swap(raw_q) * sint[...]).astype(BF16)
        key = (raw_k * cost[...] + swap(raw_k) * sint[...]).astype(BF16)
        value = qkv[:, spots[2]].astype(BF16)
        scores = contract_cols(query, key) * scale + bias[...]
        peak = jnp.max(scores, axis=-1, keepdims=True)
        powers = jnp.exp(scores - peak)
        probs = powers * (1.0 / jnp.sum(powers, axis=-1, keepdims=True))
        probs_low = probs.astype(BF16)
        out = dot_nn(probs_low, value).astype(BF16)
        attended[:, spot] = out
        grad = agrad[:, spot]
        delta = jnp.sum(grad.astype(F32) * out.astype(F32), axis=-1, keepdims=True)
        value_grad = contract_rows(probs_low, grad)
        score_low = (probs * (contract_cols(grad, value) - delta) * scale).astype(BF16)
        query_grad = dot_nn(score_low, key)
        key_grad = contract_rows(score_low, query)
        query_grad = query_grad * cost[...] - swap(query_grad) * sint[...]
        key_grad = key_grad * cost[...] - swap(key_grad) * sint[...]
        for s, g in enumerate((query_grad, key_grad, value_grad)):
            small[1:2, spots[s]] = jnp.sum(g, axis=0, keepdims=True)
            qkvlow[:, spots[s]] = g.astype(BF16)
        if h == 0:
            relay(0)
        if h == heads - 1:
            relay(1)

    spread(2, [(slice(0, wide), n1t, qkvlow), (slice(wide, ffn), ct, attended)])

    @pl.loop(0, nt)
    def _(b):
        part = pl.ds(pl.multiple_of(b * rows, rows), rows)
        first_grad = contract_cols(qkvlow[part, :], wg[2, :, :wide])
        small[2:3, :] += jnp.sum(first_grad * normed[part, :], axis=0, keepdims=True)
        small[3:4, :] += jnp.sum(first_grad, axis=0, keepdims=True)
        small[6:7, :] += jnp.sum(cg[part, :].astype(F32), axis=0, keepdims=True)
        nacc[part, :] = first_grad * gain1

    landed(0)
    small[7:8, :] = flat(fc1b_ref)

    @pl.loop(0, ffn // step)
    def _(j):
        cols = pl.ds(pl.multiple_of(j * step, step), step)
        pre = dot_nn(n2[...], wg[0, :, cols]) + small[7:8, cols]
        cdf = 0.5 * (1.0 + lax.erf(pre * (1.0 / math.sqrt(2.0))))
        hidden[:, cols] = (pre * cdf).astype(BF16)
        density = jnp.exp(-0.5 * pre * pre) * (1.0 / math.sqrt(2.0 * math.pi))
        slope[:, cols] = cdf + pre * density

    spread(1, [(slice(0, ffn), ct, hidden)])
    pass_on(2)
    landed(1)

    @pl.loop(0, ffn // step)
    def _(j):
        cols = pl.ds(pl.multiple_of(j * step, step), step)
        pre_grad = dot_nn(cg[...], wg[1, :, cols]) * slope[:, cols]
        prelow[:, cols] = pre_grad.astype(BF16)
        small[0:1, cols] = jnp.sum(pre_grad, axis=0, keepdims=True)

    spread(0, [(slice(0, ffn), n2t, prelow)])
    pass_on(1)

    @pl.loop(0, nt)
    def _(b):
        part = pl.ds(pl.multiple_of(b * rows, rows), rows)
        second_grad = contract_cols(prelow[part, :], wg[0])
        small[4:5, :] += jnp.sum(second_grad * normed[part, :], axis=0, keepdims=True)
        small[5:6, :] += jnp.sum(second_grad, axis=0, keepdims=True)
        nbuf[part, :] = (nacc[part, :] + second_grad * gain2).astype(BF16)

    for k in range(1, nt):
        peer = lax.rem(t + k, nt)
        send(nbuf.at[trows(peer)], nbufr.at[k], par_s.at[1, k], par_r.at[1, k], p, peer)
    small_all[p] = small[...]
    for k in range(1, ndp):
        send(
            small, small_all.at[p], sm_s.at[k], sm_r.at[k], lax.rem(p + k, ndp), t
        )

    @pl.loop(0, nt)
    def _(b):
        part = pl.ds(pl.multiple_of(b * rows, rows), rows)
        abuf[part, :] = (
            contract_cols(attended[part, :], wg[2, :, wide:])
            + contract_cols(hidden[part, :], wg[1])
        ).astype(BF16)

    for k in range(1, nt):
        peer = lax.rem(t + k, nt)
        send(abuf.at[trows(peer)], abufr.at[k], par_s.at[0, k], par_r.at[0, k], p, peer)
    finish(2)
    pass_on(0)

    for k in range(1, ndp):
        owner = lax.rem(p + ndp - k, ndp)
        arrive(small_all.at[owner], sm_s.at[k], sm_r.at[k])
    total = small_all[0]
    for i in range(1, ndp):
        total = total + small_all[i]
    sdp[...] = total
    sall_ref[t] = total
    for k in range(1, nt):
        peer = lax.rem(t + k, nt)
        send(sdp, sall_ref.at[t], st_s.at[k], st_r.at[k], p, peer)

    finish(1)

    grad_sum = nbuf[trows(t), :].astype(F32)
    for k in range(1, nt):
        arrive(nbufr.at[k], par_s.at[1, k], par_r.at[1, k])
        grad_sum = grad_sum + nbufr[k].astype(F32)
    value, inv_std = layer_stats(x_ref[...])
    row_mean = jnp.mean(grad_sum, axis=-1, keepdims=True)
    row_cross = jnp.mean(grad_sum * value, axis=-1, keepdims=True)
    ing_ref[...] = (
        c_ref[...].astype(F32) + inv_std * (grad_sum - row_mean - value * row_cross)
    ).astype(BF16)

    branch = abuf[trows(t), :].astype(F32)
    for k in range(1, nt):
        arrive(abufr.at[k], par_s.at[0, k], par_r.at[0, k])
        branch = branch + abufr[k].astype(F32)
    act_ref[...] = (x_ref[...].astype(F32) + branch + flat(ob_ref)).astype(BF16)

    for k in range(1, nt):
        owner = lax.rem(t + nt - k, nt)
        arrive(sall_ref.at[owner], st_s.at[k], st_r.at[k])
    finish(0)
    for copy in pending:
        copy.wait_send()


def output_kernel(
    act_ref,
    ing_ref,
    gout_ref,
    sall_ref,
    act_out,
    ing_out,
    qkv_out,
    qkvb_out,
    out_out,
    fc1_out,
    fc1b_out,
    fc2_out,
    outb_out,
    gain1_out,
    bias1_out,
    gain2_out,
    bias2_out,
):
    act_out[...] = act_ref[...]
    ing_out[...] = ing_ref[...]
    local = out_out.shape[0]
    ffn = fc2_out.shape[1]
    nt = sall_ref.shape[0]
    width = outb_out.shape[0]
    third = gout_ref[2]
    for s in range(3):
        qkv_out[s] = third[:, s * local : (s + 1) * local]
    out_out[...] = third[:, 3 * local :].T
    fc1_out[...] = gout_ref[0]
    fc2_out[...] = gout_ref[1]
    for i in range(nt):
        fc1b_out[i * ffn : (i + 1) * ffn] = sall_ref[i, 0:1, :ffn].reshape(ffn)
        for s in range(3):
            qkvb_out[s : s + 1, i * local : (i + 1) * local] = sall_ref[
                i, 1:2, s * local : (s + 1) * local
            ]
    sums = sall_ref[0, :, :width]
    for i in range(1, nt):
        sums = sums + sall_ref[i, :, :width]
    for row, ref in ((2, gain1_out), (3, bias1_out), (4, gain2_out), (5, bias2_out)):
        ref[...] = sums[row : row + 1, :].reshape(width)
    outb_out[...] = sall_ref[0, 6:7, :width].reshape(width)


def body(ndp, nt, *arrays):
    (
        layer_input,
        cotangent,
        segments,
        positions,
        norm1_gain,
        norm1_bias,
        norm2_gain,
        norm2_bias,
        qkv_weight,
        qkv_bias,
        out_weight,
        fc1_weight,
        fc1_bias,
        fc2_weight,
        out_bias,
    ) = arrays
    rows, width = layer_input.shape
    length = segments.shape[0]
    shard, _, local = qkv_weight.shape
    ffn = fc1_weight.shape[1]
    heads = local // HEAD_DIM
    if ndp % NEAR or shard % 16 or rows % 128 or ffn % 128 or 4 * local != ffn or ffn != width:
        return plain_body(*arrays)
    nz = ndp // NEAR
    wide = max(ffn, width)
    vm = pltpu.VMEM
    dma = pltpu.SemaphoreType.DMA
    spec = pl.BlockSpec(memory_space=pltpu.VMEM)
    act, ing, gout, sall = pl.pallas_call(
        functools.partial(block_kernel, ndp, nt, heads),
        out_shape=(
            jax.ShapeDtypeStruct((rows, width), BF16),
            jax.ShapeDtypeStruct((rows, width), BF16),
            jax.ShapeDtypeStruct((3, shard, ffn), F32),
            jax.ShapeDtypeStruct((nt, 8, wide), F32),
        ),
        in_specs=[spec] * 15,
        out_specs=(spec,) * 4,
        scratch_shapes=[
            vm((length, width), BF16),
            vm((length, width), BF16),
            vm((length, width), F32),
            vm((length, width), BF16),
            vm((length, width), BF16),
            vm((width, length), BF16),
            vm((width, length), BF16),
            vm((width, length), BF16),
            vm((length, HEAD_DIM), F32),
            vm((length, HEAD_DIM), F32),
            vm((length, length), F32),
            vm((3, width, ffn), BF16),
            vm((3, width, ffn), BF16),
            vm((3, nz, shard, ffn), BF16),
            vm((3, nz, shard, ffn), BF16),
            vm((3, nz, shard, ffn), BF16),
            vm((length, ffn), BF16),
            vm((length, ffn), F32),
            vm((length, ffn), BF16),
            vm((length, 3 * local), F32),
            vm((length, 3 * local), BF16),
            vm((length, local), BF16),
            vm((length, local), BF16),
            vm((length, width), F32),
            vm((length, width), BF16),
            vm((length, width), BF16),
            vm((nt, rows, width), BF16),
            vm((nt, rows, width), BF16),
            vm((8, wide), F32),
            vm((ndp, 8, wide), F32),
            vm((8, wide), F32),
            vm((shard, ffn), BF16),
            dma((2, nt)),
            dma((2, nt)),
            dma((3, nz)),
            dma((3, nz)),
            dma((3, nz)),
            dma((3, nz)),
            dma((3, nz)),
            dma((3, nz)),
            dma((3, nz)),
            dma((3, nz)),
            dma((2, nt)),
            dma((2, nt)),
            dma((ndp,)),
            dma((ndp,)),
            dma((nt,)),
            dma((nt,)),
        ],
        compiler_params=pltpu.CompilerParams(
            collective_id=0, has_side_effects=True, vmem_limit_bytes=58 * 2**20
        ),
    )(
        layer_input,
        cotangent,
        positions,
        segments,
        norm1_gain,
        norm1_bias,
        norm2_gain,
        norm2_bias,
        out_bias,
        qkv_bias,
        fc1_bias,
        fc1_weight,
        fc2_weight.T,
        qkv_weight.transpose(1, 0, 2),
        out_weight,
    )
    line = jax.ShapeDtypeStruct((width,), F32)
    outs = pl.pallas_call(
        output_kernel,
        out_shape=(
            jax.ShapeDtypeStruct((rows, width), BF16),
            jax.ShapeDtypeStruct((rows, width), BF16),
            jax.ShapeDtypeStruct((3, shard, local), F32),
            jax.ShapeDtypeStruct((3, nt * local), F32),
            jax.ShapeDtypeStruct((local, shard), F32),
            jax.ShapeDtypeStruct((shard, ffn), F32),
            jax.ShapeDtypeStruct((nt * ffn,), F32),
            jax.ShapeDtypeStruct((shard, ffn), F32),
        )
        + (line,) * 5,
        in_specs=[spec] * 4,
        out_specs=(spec,) * 13,
    )(act, ing, gout, sall)
    return (*outs[:2], outs[2].transpose(1, 0, 2), *outs[3:7], outs[7].T, *outs[8:])


def solution(mesh):
    return jax.shard_map(
        functools.partial(body, mesh.shape["dp"], mesh.shape["tensor"]),
        mesh=mesh,
        in_specs=(
            P(("dp", "tensor"), None),
            P(("dp", "tensor"), None),
            P("dp"),
            P("dp"),
            P(),
            P(),
            P(),
            P(),
            P("dp", None, "tensor"),
            P(None, "tensor"),
            P("tensor", "dp"),
            P("dp", "tensor"),
            P("tensor"),
            P("tensor", "dp"),
            P(),
        ),
        out_specs=(
            P(("dp", "tensor"), None),
            P(("dp", "tensor"), None),
            P("dp", None, "tensor"),
            P(),
            P("tensor", "dp"),
            P("dp", "tensor"),
            P(),
            P("tensor", "dp"),
            P(),
            P(),
            P(),
            P(),
            P(),
        ),
        check_vma=False,
    )
```
